32 devices in a mesh: pp: 2 (over y), cp: 4 (over z), tp: 4 (over x, core).
Axes of the slice: x: 2, y: 2, z: 4, core: 2. Of those that a mesh axis runs over, the one named last changes fastest.
Arguments:
- query_vectors: bfloat16 [2, 768, 4096], P('pp', 'cp', 'tp'), may hold values from -50 to 50
- key_vectors: bfloat16 [2, 768, 4096], P('pp', 'cp', 'tp'), may hold values from -0.5 to 0.5
- value_vectors: bfloat16 [2, 768, 4096], P('pp', 'cp', 'tp'), may hold values from -150 to 150
- section_inputs: bfloat16 [2, 768, 4096], P('pp', 'cp', 'tp'), may hold values from -6 to 6
- top_grad: bfloat16 [768, 4096], P('cp', 'tp'), may hold values from -6 to 6
- out_gains: float32 [2, 4096], P('pp', 'tp'), may hold values from 0.5 to 2
Outputs:
- section_grads: bfloat16 [2, 768, 4096], P('pp', 'cp', 'tp')
- query_grads: bfloat16 [2, 768, 4096], P('pp', 'cp', 'tp')
- key_grads: bfloat16 [2, 768, 4096], P('pp', 'cp', 'tp')
- value_grads: bfloat16 [2, 768, 4096], P('pp', 'cp', 'tp')
The draws below stay inside these ranges and needn't reach their ends.
All inputs are finite; a program needn't handle non-finite values.
Results may differ from the reference program's by a relative error of at most 0.01.
Values may be sent and summed in bfloat16 or wider, within the bound.
A program may use at most 64 MiB of HBM per device.

```python
import math
import jax
import jax.numpy as jnp
from jax import lax

HEADS = 32
HEAD = 128
WIDTH = 4096
TOK_DEV = 192
TOKENS = 768
LAYERS = 2


def draw_query_vectors(key, part):
    base_key, scale_key = jax.random.split(jax.random.fold_in(key, 11))
    base = jnp.clip(jax.random.normal(base_key, (LAYERS, TOKENS, WIDTH), jnp.float32), -5.0, 5.0)
    row_scale = jnp.exp(jax.random.uniform(scale_key, (LAYERS, TOKENS, 1), jnp.float32, 0.0, math.log(10.0)))
    return (base * row_scale).astype(jnp.bfloat16)


def draw_value_vectors(key, part):
    base_key, column_key = jax.random.split(jax.random.fold_in(key, 23), 2)
    head_index = (jnp.arange(WIDTH) // HEAD).astype(jnp.float32)
    rising = jnp.exp(head_index * (math.log(3.0) / max(HEADS - 1, 1)))
    column_scale = jnp.exp(jax.random.uniform(column_key, (LAYERS, 1, WIDTH), jnp.float32, 0.0, math.log(10.0))) * rising
    base = jnp.clip(jax.random.normal(base_key, (LAYERS, TOKENS, WIDTH), jnp.float32), -5.0, 5.0)
    return (base * column_scale).astype(jnp.bfloat16)


def shard_levels(key, extent, cuts, low, largest):
    def one(position, blocks):
        heights = jax.random.uniform(jax.random.fold_in(jax.random.fold_in(key, 6), position), (blocks,), jnp.float32, low / len(cuts), largest / len(cuts))
        return jnp.repeat(jnp.exp(heights), extent[position] // blocks).reshape((-1,) + (1,) * (len(extent) - position - 1))

    level = one(*cuts[0])
    for cut in cuts[1:]:
        level = level * one(*cut)
    return level


def centred(key, extent, scale, most, shards=(), held_as=jnp.bfloat16):
    values = scale * jax.random.normal(key, extent, jnp.float32)
    if shards:
        values = values * shard_levels(key, extent, shards, -0.22, 0.18)
    return jnp.clip(values, -most, most).astype(held_as)


def setup_inputs(seed: int = 0) -> dict:
    splits = jax.random.split(jax.random.key(seed), 7)
    return {
        "query_vectors": draw_query_vectors(jax.random.fold_in(splits[6], 71), 0),
        "key_vectors": centred(splits[1], (LAYERS, TOKENS, WIDTH), HEAD ** -0.5, 0.5, ((0, 2), (1, 4), (2, 4))),
        "value_vectors": draw_value_vectors(jax.random.fold_in(splits[6], 71), 0),
        "section_inputs": centred(splits[3], (LAYERS, TOKENS, WIDTH), 1.5, 6.0, ((0, 2), (1, 4), (2, 4))),
        "top_grad": centred(splits[4], (TOKENS, WIDTH), 1.0, 6.0, ((0, 4), (1, 4))),
        "out_gains": jnp.clip(jnp.exp(math.log(2.0) - 1.3862944 * jax.random.uniform(splits[5], (LAYERS, WIDTH), jnp.float32) ** shard_levels(splits[5], (LAYERS, WIDTH), ((0, 2), (1, 4)), -0.2, 0.2)), 0.5, 2.0),
    }


EPSILON = 1e-06

def rounded(array):
    return lax.optimization_barrier(array.astype(jnp.bfloat16)).astype(jnp.float32)

def layer_grads(query_layer, key_layer, value_layer, section_input, out_gain, top_grad, later_product):
    blocks = TOKENS // TOK_DEV
    block_shape = (blocks, TOK_DEV, HEADS, HEAD)
    query_blocks = query_layer.astype(jnp.float32).reshape(block_shape)
    key_blocks = key_layer.astype(jnp.float32).reshape(block_shape)
    value_blocks = value_layer.astype(jnp.float32).reshape(block_shape)
    causal = jnp.arange(TOK_DEV)[:, None] >= jnp.arange(TOK_DEV)[None, :]
    local_state = jnp.einsum('bthd,bthe->bhde', key_blocks, value_blocks)
    running = jnp.cumsum(local_state, axis=0)
    prefix = rounded(jnp.concatenate([jnp.zeros_like(local_state[:1]), running[:-1]], axis=0))
    scores = rounded(jnp.where(causal, jnp.einsum('bthd,bshd->bhts', query_blocks, key_blocks), 0.0))
    attention = jnp.einsum('bhts,bshe->bthe', scores, value_blocks) + jnp.einsum('bthd,bhde->bthe', query_blocks, prefix)
    attention = attention.reshape(TOKENS, WIDTH)
    scale_root = jnp.sqrt(lax.optimization_barrier(jnp.mean(attention * attention, axis=1, keepdims=True)) + EPSILON)
    normed = attention / scale_root
    sigmoid_gate = jax.nn.sigmoid(section_input.astype(jnp.float32))
    factor = 1.0 + out_gain * normed * sigmoid_gate * (1.0 - sigmoid_gate)
    incoming_grad = top_grad.astype(jnp.float32) * later_product
    section_grad = (incoming_grad * factor).astype(jnp.bfloat16)
    normed_grad = incoming_grad * out_gain * sigmoid_gate
    inner_mean = lax.optimization_barrier(jnp.mean(normed_grad * normed, axis=1, keepdims=True))
    attention_grad = rounded((normed_grad - normed * inner_mean) / scale_root).reshape(block_shape)
    grad_state = jnp.einsum('bthd,bthe->bhde', query_blocks, attention_grad)
    behind = jnp.cumsum(grad_state[::-1], axis=0)[::-1]
    suffix = rounded(jnp.concatenate([behind[1:], jnp.zeros_like(grad_state[:1])], axis=0))
    score_grad = rounded(jnp.where(causal, jnp.einsum('bthe,bshe->bhts', attention_grad, value_blocks), 0.0))
    query_grad = jnp.einsum('bhts,bshd->bthd', score_grad, key_blocks) + jnp.einsum('bthe,bhde->bthd', attention_grad, prefix)
    key_grad = jnp.einsum('bhts,bthd->bshd', score_grad, query_blocks) + jnp.einsum('bshe,bhde->bshd', value_blocks, suffix)
    value_grad = jnp.einsum('bhts,bthe->bshe', scores, attention_grad) + jnp.einsum('bshd,bhde->bshe', key_blocks, suffix)
    query_grad = query_grad.reshape(TOKENS, WIDTH).astype(jnp.bfloat16)
    key_grad = key_grad.reshape(TOKENS, WIDTH).astype(jnp.bfloat16)
    value_grad = value_grad.reshape(TOKENS, WIDTH).astype(jnp.bfloat16)
    return (factor, section_grad, query_grad, key_grad, value_grad)

def reference(query_vectors, key_vectors, value_vectors, section_inputs, top_grad, out_gains):
    later_product = jnp.ones((TOKENS, WIDTH), jnp.float32)
    section_list = []
    query_list = []
    key_list = []
    value_list = []
    for section_index in range(LAYERS - 1, -1, -1):
        factor, section_grad, query_grad, key_grad, value_grad = layer_grads(query_vectors[section_index], key_vectors[section_index], value_vectors[section_index], section_inputs[section_index], out_gains[section_index][None, :], top_grad, later_product)
        section_list.insert(0, section_grad)
        query_list.insert(0, query_grad)
        key_list.insert(0, key_grad)
        value_list.insert(0, value_grad)
        later_product = later_product * factor
    return (jnp.stack(section_list), jnp.stack(query_list), jnp.stack(key_list), jnp.stack(value_list))
```

```python
import functools

import jax
import jax.numpy as jnp
from jax import lax
from jax.experimental import pallas as pl
from jax.experimental.pallas import tpu as pltpu
from jax.sharding import PartitionSpec as P

HEAD = 128
LANES = 128
EPSILON = 1e-06
PIECES = 4
LEAD = 2
TRAIL = 2
VMEM_LIMIT = 24 << 20
MESH = pl.DeviceIdType.MESH
F32 = jnp.float32
BF16 = jnp.bfloat16


def dot(a, b, a_dim, b_dim):
    return lax.dot_general(a, b, (((a_dim,), (b_dim,)), ((), ())), preferred_element_type=F32)


def kernel(
    sizes,
    q_hbm, k_hbm, v_hbm, x_hbm, top_hbm, gain_hbm,
    outs,
    q, k, v, x, top, gain,
    pre_in, pre_out, suf_in, suf_out, states, scores, att, ng, gate, ag, b_out, b_in,
    rows_out, rows_in, inv_out, inv_in,
    in_sem, chain_send, chain_recv,
    b_send, b_recv, row_send, row_recv, inv_send, inv_recv,
):
    layers, blocks, shards = sizes
    p = lax.axis_index("pp") if layers > 1 else jnp.int32(0)
    c = lax.axis_index("cp") if blocks > 1 else jnp.int32(0)
    t = lax.axis_index("tp") if shards > 1 else jnp.int32(0)
    rows, width = q.shape
    sec, qg, kg, vg = (outs.at[i] for i in range(4))
    heads = width // HEAD
    padded = rows_out.shape[2]
    total_width = width * shards

    def part(i):
        return slice(i * (HEAD // PIECES), (i + 1) * (HEAD // PIECES))

    def cols(h):
        return slice(h * HEAD, (h + 1) * HEAD)

    loads = [
        pltpu.make_async_copy(k_hbm.at[0], k, in_sem.at[0]),
        pltpu.make_async_copy(v_hbm.at[0], v, in_sem.at[1]),
        pltpu.make_async_copy(q_hbm.at[0], q, in_sem.at[2]),
        pltpu.make_async_copy(x_hbm.at[0], x, in_sem.at[3]),
        pltpu.make_async_copy(gain_hbm, gain, in_sem.at[4]),
        pltpu.make_async_copy(top_hbm, top, in_sem.at[5]),
    ]
    for load in loads[:2]:
        load.start()

    barrier = pltpu.get_barrier_semaphore()

    @pl.when(c > 0)
    def _():
        pl.semaphore_signal(barrier, inc=1, device_id={"cp": c - 1}, device_id_type=MESH)

    @pl.when(c < blocks - 1)
    def _():
        pl.semaphore_signal(barrier, inc=1, device_id={"cp": c + 1}, device_id_type=MESH)

    for d in range(1, shards):
        pl.semaphore_signal(
            barrier, inc=1, device_id={"tp": lax.rem(t + d, shards)}, device_id_type=MESH
        )
    for d in range(1, layers):
        pl.semaphore_signal(
            barrier, inc=1, device_id={"pp": lax.rem(p + d, layers)}, device_id_type=MESH
        )

    @pl.when(c == 0)
    def _():
        pre_in[...] = jnp.zeros_like(pre_in)

    @pl.when(c == blocks - 1)
    def _():
        suf_in[...] = jnp.zeros_like(suf_in)

    for d in range(1, layers):

        @pl.when(p + d >= layers)
        def _():
            b_in[d - 1] = jnp.zeros(b_in.shape[1:], b_in.dtype)
            inv_in[d - 1] = jnp.zeros(inv_in.shape[1:], inv_in.dtype)

    def pre_copy(h, i):
        return pltpu.make_async_remote_copy(
            src_ref=pre_out.at[h, part(i)], dst_ref=pre_in.at[h, part(i)],
            send_sem=chain_send.at[0], recv_sem=chain_recv.at[h, i],
            device_id={"cp": c + 1}, device_id_type=MESH,
        )

    def suf_copy(h, i):
        return pltpu.make_async_remote_copy(
            src_ref=suf_out.at[h, part(i)], dst_ref=suf_in.at[h, part(i)],
            send_sem=chain_send.at[1], recv_sem=chain_recv.at[h, i],
            device_id={"cp": c - 1}, device_id_type=MESH,
        )

    def b_copy(d, h):
        return pltpu.make_async_remote_copy(
            src_ref=b_out.at[h], dst_ref=b_in.at[d - 1, h],
            send_sem=b_send.at[d - 1], recv_sem=b_recv.at[d - 1, h],
            device_id={"pp": p - d}, device_id_type=MESH,
        )

    def inv_copy(d):
        return pltpu.make_async_remote_copy(
            src_ref=inv_out, dst_ref=inv_in.at[d - 1],
            send_sem=inv_send.at[d - 1], recv_sem=inv_recv.at[d - 1],
            device_id={"pp": p - d}, device_id_type=MESH,
        )

    def row_copy(i, d):
        return pltpu.make_async_remote_copy(
            src_ref=rows_out.at[i], dst_ref=rows_in.at[i, d - 1],
            send_sem=row_send.at[i], recv_sem=row_recv.at[i],
            device_id={"tp": lax.rem(t + d, shards)}, device_id_type=MESH,
        )

    def to_row(partial):
        if padded > rows:
            fill = jnp.zeros((padded - rows, LANES), F32)
            partial = jnp.concatenate([partial, fill], axis=0)
        return jnp.broadcast_to(jnp.sum(partial.T, axis=0, keepdims=True), (8, padded))

    def to_col(row):
        return jnp.broadcast_to(row[0:1], (LANES, padded)).T[:rows]

    def row_start(i, partials):
        ids = lax.broadcasted_iota(jnp.int32, (8, padded), 0)
        packed = to_row(partials[0])
        for j in range(1, len(partials)):
            packed = jnp.where(ids == j, to_row(partials[j]), packed)
        rows_out[i] = packed
        for d in range(1, shards):
            row_copy(i, d).start()

    def row_all(i):
        return pltpu.make_async_remote_copy(
            src_ref=rows_in.at[i], dst_ref=rows_in.at[i],
            send_sem=row_send.at[i], recv_sem=row_recv.at[i],
            device_id={"tp": lax.rem(t + 1, shards)}, device_id_type=MESH,
        )

    def row_finish(i):
        total = rows_out[i]
        if shards > 1:
            row_all(i).wait_recv()
        for d in range(1, shards):
            total = total + rows_in[i, d - 1]
        return total

    def row_sent(i):
        if shards > 1:
            row_all(i).wait_send()

    causal = lax.broadcasted_iota(jnp.int32, (rows, rows), 0) >= lax.broadcasted_iota(
        jnp.int32, (rows, rows), 1
    )

    def forward(copy, arrived, sent, h, inner, outer):
        @pl.when(inner)
        def _():
            for i in range(PIECES):
                copy(h, i).wait_recv()
                total = arrived[h, part(i)].astype(F32) + states[h, part(i)]
                sent[h, part(i)] = total.astype(BF16)
                copy(h, i).start()

        @pl.when(outer)
        def _():
            for i in range(PIECES):
                copy(h, i).wait_recv()

    def first(copy, sent, h):
        for i in range(PIECES):
            sent[h, part(i)] = states[h, part(i)].astype(BF16)
            copy(h, i).start()

    def local(h):
        query, value = q[:, cols(h)], v[:, cols(h)]
        score = jnp.where(causal, dot(query, k[:, cols(h)], 1, 1), 0.0).astype(BF16)
        scores[h] = score
        att[:, cols(h)] = dot(score, value, 1, 0)
        gate[:, cols(h)] = jax.nn.sigmoid(x[:, cols(h)].astype(F32))

    loads[0].wait()
    loads[1].wait()
    for load in loads[2:]:
        load.start()
    states[0] = dot(k[:, cols(0)], v[:, cols(0)], 0, 0)
    partners = (shards - 1) + (layers - 1)
    pl.semaphore_wait(
        barrier, partners + jnp.where(c > 0, 1, 0) + jnp.where(c < blocks - 1, 1, 0)
    )
    for h in range(heads):
        if h > 0:
            states[h] = dot(k[:, cols(h)], v[:, cols(h)], 0, 0)
        if blocks > 1:

            @pl.when(c == 0)
            def _():
                first(pre_copy, pre_out, h)

    for load in loads[2:]:
        load.wait()
    lead = min(LEAD, heads) if blocks > 1 else heads
    for h in range(lead):
        local(h)
    if lead < heads:

        @pl.when(c != 1)
        def _():
            for h in range(lead, heads):
                local(h)

    merged = layers <= 2
    squares = jnp.zeros((rows, LANES), F32)
    firsts = jnp.zeros((rows, LANES), F32)
    for h in range(heads):
        if blocks > 1:
            forward(pre_copy, pre_in, pre_out, h, (c > 0) & (c < blocks - 1), (c > 0) & (c == blocks - 1))
        attention = att[:, cols(h)] + dot(q[:, cols(h)], pre_in[h], 1, 0)
        att[:, cols(h)] = attention
        squares = squares + attention * attention
        sig = gate[:, cols(h)]
        if merged:
            weighted = top[:, cols(h)].astype(F32) * (gain[:, cols(h)] * sig)
            ng[:, cols(h)] = weighted
            firsts = firsts + weighted * attention
        if layers > 1:
            b_out[h] = (attention * (gain[:, cols(h)] * sig * (1.0 - sig))).astype(BF16)
        for d in range(1, layers):

            @pl.when(p >= d)
            def _():
                b_copy(d, h).start()

        if h + lead < heads:

            @pl.when(c == 1)
            def _():
                local(h + lead)

    row_start(0, (squares, firsts))
    sums = row_finish(0)
    inv_row = 1.0 / jnp.sqrt(sums[0:1] / total_width + EPSILON)
    inv_out[...] = jnp.broadcast_to(inv_row, inv_out.shape)
    for d in range(1, layers):

        @pl.when(p >= d)
        def _():
            inv_copy(d).start()

    inv = to_col(inv_row)

    def wait_inv():
        for d in range(1, layers):

            @pl.when(p + d < layers)
            def _():
                inv_copy(d).wait_recv()

    def wait_b(some):
        for d in range(1, layers):

            @pl.when(p + d < layers)
            def _():
                for h in some:
                    b_copy(d, h).wait_recv()

    def later(h, later_inv):
        incoming = top[:, cols(h)].astype(F32)
        for d in range(1, layers):
            incoming = incoming * (1.0 + b_in[d - 1, h].astype(F32) * later_inv[d - 1])
        return incoming

    if merged:
        mean_row = sums[1:2]
        if layers > 1:
            seconds = jnp.zeros((rows, LANES), F32)
            for h in range(heads):
                wait_b([h])
                seconds = seconds + ng[:, cols(h)] * att[:, cols(h)] * b_in[0, h].astype(F32)

            @pl.when(p < layers - 1)
            def _():
                row_start(1, (seconds,))
                wait_inv()
                total = row_finish(1)
                row_sent(1)
                rows_out[1] = total

            @pl.when(p == layers - 1)
            def _():
                rows_out[1] = jnp.zeros(rows_out.shape[1:], F32)

            mean_row = mean_row + inv_in[0, 0:1] * rows_out[1, 0:1]
        mean_row = mean_row * inv_row
        later_inv = [to_col(inv_in[d - 1]) for d in range(1, layers)]
    else:
        wait_inv()
        later_inv = [to_col(inv_in[d - 1]) for d in range(1, layers)]
        products = jnp.zeros((rows, LANES), F32)
        for h in range(heads):
            wait_b([h])
            weighted = later(h, later_inv) * (gain[:, cols(h)] * gate[:, cols(h)])
            ng[:, cols(h)] = weighted
            products = products + weighted * att[:, cols(h)] * inv
        row_start(1, (products,))
        mean_row = row_finish(1)
    mean = to_col(mean_row / total_width)
    for h in range(heads):
        weighted = ng[:, cols(h)]
        if merged and layers > 1:
            weighted = weighted * (1.0 + b_in[0, h].astype(F32) * later_inv[0])
        grad = ((weighted - att[:, cols(h)] * inv * mean) * inv).astype(BF16)
        ag[:, cols(h)] = grad
        states[h] = dot(q[:, cols(h)], grad, 0, 0)
        if blocks > 1:

            @pl.when(c == blocks - 1)
            def _():
                first(suf_copy, suf_out, h)

    def inner_grads(h):
        sig = gate[:, cols(h)]
        slope = gain[:, cols(h)] * sig * (1.0 - sig)
        factor = 1.0 + att[:, cols(h)] * inv * slope
        sec[:, cols(h)] = (later(h, later_inv) * factor).astype(BF16)
        query, key, value = q[:, cols(h)], k[:, cols(h)], v[:, cols(h)]
        grad = ag[:, cols(h)]
        score_grad = jnp.where(causal, dot(grad, value, 1, 1), 0.0).astype(BF16)
        query_grad = dot(score_grad, key, 1, 0) + dot(grad, pre_in[h], 1, 1)
        qg[:, cols(h)] = query_grad.astype(BF16)
        att[:, cols(h)] = dot(score_grad, query, 0, 0)
        ng[:, cols(h)] = dot(scores[h], grad, 0, 0)

    trail = max(heads - TRAIL, 0) if blocks > 1 else heads
    for h in range(trail):
        inner_grads(h)
    if trail < heads:

        @pl.when(c != blocks - 2)
        def _():
            for h in range(trail, heads):
                inner_grads(h)

    for h in range(heads):
        if blocks > 1:
            forward(suf_copy, suf_in, suf_out, h, (c < blocks - 1) & (c > 0), (c < blocks - 1) & (c == 0))
        if trail + h < heads:

            @pl.when(c == blocks - 2)
            def _():
                inner_grads(trail + h)

        suffix = suf_in[h]
        key_grad = att[:, cols(h)] + dot(v[:, cols(h)], suffix, 1, 1)
        kg[:, cols(h)] = key_grad.astype(BF16)
        value_grad = ng[:, cols(h)] + dot(k[:, cols(h)], suffix, 1, 0)
        vg[:, cols(h)] = value_grad.astype(BF16)

    if blocks > 1:

        @pl.when(c < blocks - 1)
        def _():
            pltpu.make_async_remote_copy(
                src_ref=pre_out, dst_ref=pre_in,
                send_sem=chain_send.at[0], recv_sem=chain_recv.at[0, 0],
                device_id={"cp": c + 1}, device_id_type=MESH,
            ).wait_send()

        @pl.when(c > 0)
        def _():
            pltpu.make_async_remote_copy(
                src_ref=suf_out, dst_ref=suf_in,
                send_sem=chain_send.at[1], recv_sem=chain_recv.at[0, 0],
                device_id={"cp": c - 1}, device_id_type=MESH,
            ).wait_send()

    for d in range(1, layers):

        @pl.when(p >= d)
        def _():
            inv_copy(d).wait_send()
            pltpu.make_async_remote_copy(
                src_ref=b_out, dst_ref=b_in.at[d - 1],
                send_sem=b_send.at[d - 1], recv_sem=b_recv.at[d - 1, 0],
                device_id={"pp": p - d}, device_id_type=MESH,
            ).wait_send()

    row_sent(0)
    if not merged:
        row_sent(1)


def write_kernel(outs, sec_hbm, qg_hbm, kg_hbm, vg_hbm, sem):
    rows = outs.shape[1]
    step = rows // 4 if rows % 32 == 0 else rows
    dsts = (sec_hbm, qg_hbm, kg_hbm, vg_hbm)
    for i, dst in enumerate(dsts):
        for r in range(0, rows, step):
            pltpu.make_async_copy(
                outs.at[i, r : r + step], dst.at[0, r : r + step], sem.at[i]
            ).start()
    for i, dst in enumerate(dsts):
        pltpu.make_async_copy(outs.at[i], dst.at[0], sem.at[i]).wait()


def on_device(sizes, q, k, v, x, top, gains):
    layers, blocks, shards = sizes
    rows, width = q.shape[1:]
    heads = width // HEAD
    padded = -(-rows // LANES) * LANES
    others, peers = max(layers - 1, 1), max(shards - 1, 1)
    wide = pltpu.VMEM((rows, width), BF16)
    wide32 = pltpu.VMEM((rows, width), F32)
    square = pltpu.VMEM((heads, HEAD, HEAD), BF16)
    dma = pltpu.SemaphoreType.DMA
    out = jax.ShapeDtypeStruct((1, rows, width), BF16)
    q, k, v, x, top, gains = (
        pltpu.with_memory_space_constraint(a, pltpu.HBM) for a in (q, k, v, x, top, gains)
    )
    outs = pl.pallas_call(
        functools.partial(kernel, sizes),
        out_shape=jax.ShapeDtypeStruct((4, rows, width), BF16),
        in_specs=[pl.BlockSpec(memory_space=pltpu.HBM)] * 6,
        out_specs=pl.BlockSpec(memory_space=pltpu.VMEM),
        scratch_shapes=[
            wide, wide, wide, wide, wide, pltpu.VMEM((1, width), F32),
            square, square, square, square,
            pltpu.VMEM((heads, HEAD, HEAD), F32),
            pltpu.VMEM((heads, rows, rows), BF16),
            wide32, wide32, wide32, wide,
            pltpu.VMEM((heads, rows, HEAD), BF16),
            pltpu.VMEM((others, heads, rows, HEAD), BF16),
            pltpu.VMEM((2, 8, padded), F32),
            pltpu.VMEM((2, peers, 8, padded), F32),
            pltpu.VMEM((8, padded), F32),
            pltpu.VMEM((others, 8, padded), F32),
            dma((6,)),
            dma((2,)), dma((heads, PIECES)),
            dma((others,)), dma((others, heads)),
            dma((2,)), dma((2,)),
            dma((others,)), dma((others,)),
        ],
        compiler_params=pltpu.CompilerParams(collective_id=0, has_side_effects=True, vmem_limit_bytes=VMEM_LIMIT),
    )(q, k, v, x, top, gains)
    return pl.pallas_call(
        write_kernel,
        out_shape=(out,) * 4,
        in_specs=[pl.BlockSpec(memory_space=pltpu.VMEM)],
        out_specs=(pl.BlockSpec(memory_space=pl.ANY),) * 4,
        scratch_shapes=[dma((4,))],
        compiler_params=pltpu.CompilerParams(vmem_limit_bytes=1 << 20),
    )(outs)


def solution(mesh):
    sizes = (mesh.shape["pp"], mesh.shape["cp"], mesh.shape["tp"])
    part = P("pp", "cp", "tp")
    return jax.shard_map(
        functools.partial(on_device, sizes),
        mesh=mesh,
        in_specs=(part, part, part, part, P("cp", "tp"), P("pp", "tp")),
        out_specs=(part, part, part, part),
        check_vma=False,
    )
```

```python
import functools

import jax
import jax.numpy as jnp
from jax import lax
from jax.experimental import pallas as pl
from jax.experimental.pallas import tpu as pltpu
from jax.sharding import PartitionSpec as P

HEAD = 128
LANES = 128
EPSILON = 1e-06
PIECES = 4
LEAD = 2
TRAIL = 2
SWAPPED = (3, 5)
VMEM_LIMIT = 24 << 20
MESH = pl.DeviceIdType.MESH
F32 = jnp.float32
BF16 = jnp.bfloat16


def dot(a, b, a_dim, b_dim):
    return lax.dot_general(a, b, (((a_dim,), (b_dim,)), ((), ())), preferred_element_type=F32)


def swapped_heads(heads):
    return [h for h in SWAPPED if h < heads]


def kernel(
    sizes,
    q_hbm, k_hbm, v_hbm, x_hbm, top_hbm, gain_hbm,
    outs,
    q, k, v, x, top, gain,
    pre_in, pre_out, suf_in, suf_out, states, scores, att, ng, gate, ag, b_out, b_in,
    rows_out, rows_in, inv_out, inv_in, z_out, z_in, mix_out, mix_in,
    in_sem, chain_send, chain_recv,
    b_send, b_recv, row_send, row_recv, inv_send, inv_recv, mix_sem, z_sem,
):
    layers, blocks, shards = sizes
    p = lax.axis_index("pp") if layers > 1 else jnp.int32(0)
    c = lax.axis_index("cp") if blocks > 1 else jnp.int32(0)
    t = lax.axis_index("tp") if shards > 1 else jnp.int32(0)
    rows, width = q.shape
    sec, qg, kg, vg = (outs.at[i] for i in range(4))
    heads = width // HEAD
    padded = rows_out.shape[2]
    swapped = swapped_heads(heads) if layers == 2 else []
    paired = len(swapped) > 0
    order = [h for h in range(heads) if h not in swapped] + swapped
    total_width = width * shards

    def part(i):
        return slice(i * (HEAD // PIECES), (i + 1) * (HEAD // PIECES))

    def cols(h):
        return slice(h * HEAD, (h + 1) * HEAD)

    loads = [
        pltpu.make_async_copy(k_hbm.at[0], k, in_sem.at[0]),
        pltpu.make_async_copy(v_hbm.at[0], v, in_sem.at[1]),
        pltpu.make_async_copy(q_hbm.at[0], q, in_sem.at[2]),
        pltpu.make_async_copy(x_hbm.at[0], x, in_sem.at[3]),
        pltpu.make_async_copy(gain_hbm, gain, in_sem.at[4]),
        pltpu.make_async_copy(top_hbm, top, in_sem.at[5]),
    ]
    for load in loads[:2]:
        load.start()

    barrier = pltpu.get_barrier_semaphore()

    @pl.when(c > 0)
    def _():
        pl.semaphore_signal(barrier, inc=1, device_id={"cp": c - 1}, device_id_type=MESH)

    @pl.when(c < blocks - 1)
    def _():
        pl.semaphore_signal(barrier, inc=1, device_id={"cp": c + 1}, device_id_type=MESH)

    for d in range(1, shards):
        pl.semaphore_signal(
            barrier, inc=1, device_id={"tp": lax.rem(t + d, shards)}, device_id_type=MESH
        )
    for d in range(1, layers):
        pl.semaphore_signal(
            barrier, inc=1, device_id={"pp": lax.rem(p + d, layers)}, device_id_type=MESH
        )

    @pl.when(c == 0)
    def _():
        pre_in[...] = jnp.zeros_like(pre_in)

    @pl.when(c == blocks - 1)
    def _():
        suf_in[...] = jnp.zeros_like(suf_in)

    for d in range(1, layers):

        @pl.when(p + d >= layers)
        def _():
            b_in[d - 1] = jnp.zeros(b_in.shape[1:], b_in.dtype)
            inv_in[d - 1] = jnp.zeros(inv_in.shape[1:], inv_in.dtype)

    def pre_copy(h, i):
        return pltpu.make_async_remote_copy(
            src_ref=pre_out.at[h, part(i)], dst_ref=pre_in.at[h, part(i)],
            send_sem=chain_send.at[0], recv_sem=chain_recv.at[h, i],
            device_id={"cp": c + 1}, device_id_type=MESH,
        )

    def suf_copy(h, i):
        return pltpu.make_async_remote_copy(
            src_ref=suf_out.at[h, part(i)], dst_ref=suf_in.at[h, part(i)],
            send_sem=chain_send.at[1], recv_sem=chain_recv.at[h, i],
            device_id={"cp": c - 1}, device_id_type=MESH,
        )

    def b_copy(d, h):
        return pltpu.make_async_remote_copy(
            src_ref=b_out.at[h], dst_ref=b_in.at[d - 1, h],
            send_sem=b_send.at[d - 1], recv_sem=b_recv.at[d - 1, h],
            device_id={"pp": p - d}, device_id_type=MESH,
        )

    def inv_copy(d):
        return pltpu.make_async_remote_copy(
            src_ref=inv_out, dst_ref=inv_in.at[d - 1],
            send_sem=inv_send.at[d - 1], recv_sem=inv_recv.at[d - 1],
            device_id={"pp": p - d}, device_id_type=MESH,
        )

    def z_copy(j):
        return pltpu.make_async_remote_copy(
            src_ref=z_out.at[j], dst_ref=z_in.at[j],
            send_sem=z_sem.at[0], recv_sem=z_sem.at[1],
            device_id={"pp": p + 1}, device_id_type=MESH,
        )

    def z_all():
        return pltpu.make_async_remote_copy(
            src_ref=z_out, dst_ref=z_in,
            send_sem=z_sem.at[0], recv_sem=z_sem.at[1],
            device_id={"pp": p + 1}, device_id_type=MESH,
        )

    def mix_copy(e):
        return pltpu.make_async_remote_copy(
            src_ref=mix_out, dst_ref=mix_in.at[e],
            send_sem=mix_sem.at[0], recv_sem=mix_sem.at[1],
            device_id={"pp": p - 1, "tp": lax.rem(t + e, shards)}, device_id_type=MESH,
        )

    def mix_all():
        return pltpu.make_async_remote_copy(
            src_ref=mix_in, dst_ref=mix_in,
            send_sem=mix_sem.at[0], recv_sem=mix_sem.at[1],
            device_id={"pp": p - 1}, device_id_type=MESH,
        )

    def row_copy(i, d):
        return pltpu.make_async_remote_copy(
            src_ref=rows_out.at[i], dst_ref=rows_in.at[i, d - 1],
            send_sem=row_send.at[i], recv_sem=row_recv.at[i],
            device_id={"tp": lax.rem(t + d, shards)}, device_id_type=MESH,
        )

    def to_row(partial):
        if padded > rows:
            fill = jnp.zeros((padded - rows, LANES), F32)
            partial = jnp.concatenate([partial, fill], axis=0)
        return jnp.broadcast_to(jnp.sum(partial.T, axis=0, keepdims=True), (8, padded))

    def to_col(row):
        return jnp.broadcast_to(row[0:1], (LANES, padded)).T[:rows]

    def row_start(i, partials):
        ids = lax.broadcasted_iota(jnp.int32, (8, padded), 0)
        packed = to_row(partials[0])
        for j in range(1, len(partials)):
            packed = jnp.where(ids == j, to_row(partials[j]), packed)
        rows_out[i] = packed
        for d in range(1, shards):
            row_copy(i, d).start()

    def row_all(i):
        return pltpu.make_async_remote_copy(
            src_ref=rows_in.at[i], dst_ref=rows_in.at[i],
            send_sem=row_send.at[i], recv_sem=row_recv.at[i],
            device_id={"tp": lax.rem(t + 1, shards)}, device_id_type=MESH,
        )

    def row_finish(i):
        total = rows_out[i]
        if shards > 1:
            row_all(i).wait_recv()
        for d in range(1, shards):
            total = total + rows_in[i, d - 1]
        return total

    def row_sent(i):
        if shards > 1:
            row_all(i).wait_send()

    causal = lax.broadcasted_iota(jnp.int32, (rows, rows), 0) >= lax.broadcasted_iota(
        jnp.int32, (rows, rows), 1
    )

    def forward(copy, arrived, sent, h, inner, outer):
        @pl.when(inner)
        def _():
            for i in range(PIECES):
                copy(h, i).wait_recv()
                total = arrived[h, part(i)].astype(F32) + states[h, part(i)]
                sent[h, part(i)] = total.astype(BF16)
                copy(h, i).start()

        @pl.when(outer)
        def _():
            for i in range(PIECES):
                copy(h, i).wait_recv()

    def first(copy, sent, h):
        for i in range(PIECES):
            sent[h, part(i)] = states[h, part(i)].astype(BF16)
            copy(h, i).start()

    def local(h):
        query, value = q[:, cols(h)], v[:, cols(h)]
        score = jnp.where(causal, dot(query, k[:, cols(h)], 1, 1), 0.0).astype(BF16)
        scores[h] = score
        att[:, cols(h)] = dot(score, value, 1, 0)
        gate[:, cols(h)] = jax.nn.sigmoid(x[:, cols(h)].astype(F32))

    loads[0].wait()
    loads[1].wait()
    for load in loads[2:]:
        load.start()
    states[0] = dot(k[:, cols(0)], v[:, cols(0)], 0, 0)
    partners = (shards - 1) + (layers - 1)
    pl.semaphore_wait(
        barrier, partners + jnp.where(c > 0, 1, 0) + jnp.where(c < blocks - 1, 1, 0)
    )
    for h in range(heads):
        if h > 0:
            states[h] = dot(k[:, cols(h)], v[:, cols(h)], 0, 0)
        if blocks > 1:

            @pl.when(c == 0)
            def _():
                first(pre_copy, pre_out, h)

    for load in loads[2:]:
        load.wait()
    lead = min(LEAD, heads) if blocks > 1 else heads
    for h in range(lead):
        local(h)
    if lead < heads:

        @pl.when(c != 1)
        def _():
            for h in range(lead, heads):
                local(h)

    merged = layers == 1 or paired
    squares = jnp.zeros((rows, LANES), F32)
    firsts = jnp.zeros((rows, LANES), F32)
    for h in range(heads):
        if blocks > 1:
            forward(pre_copy, pre_in, pre_out, h, (c > 0) & (c < blocks - 1), (c > 0) & (c == blocks - 1))
        attention = att[:, cols(h)] + dot(q[:, cols(h)], pre_in[h], 1, 0)
        att[:, cols(h)] = attention
        squares = squares + attention * attention
        sig = gate[:, cols(h)]
        if merged:
            weighted = top[:, cols(h)].astype(F32) * (gain[:, cols(h)] * sig)
            ng[:, cols(h)] = weighted
            firsts = firsts + weighted * attention
        if layers > 1:
            b_out[h] = (attention * (gain[:, cols(h)] * sig * (1.0 - sig))).astype(BF16)
        if h in swapped:

            @pl.when(p == 0)
            def _():
                z_out[swapped.index(h)] = (weighted * attention).astype(BF16)
                z_copy(swapped.index(h)).start()

        else:
            for d in range(1, layers):

                @pl.when(p >= d)
                def _():
                    b_copy(d, h).start()

        if h + lead < heads:

            @pl.when(c == 1)
            def _():
                local(h + lead)

    row_start(0, (squares, firsts))
    if paired:

        @pl.when(p == 1)
        def _():
            seconds = jnp.zeros((rows, LANES), F32)
            z_all().wait_recv()
            for j, h in enumerate(swapped):
                seconds = seconds + z_in[j].astype(F32) * b_out[h].astype(F32)
            ids = lax.broadcasted_iota(jnp.int32, (8, padded), 0)
            mix_out[...] = jnp.where(ids == 1, to_row(seconds), rows_out[0])
            for e in range(shards):
                mix_copy(e).start()

    sums = row_finish(0)
    if paired:

        @pl.when(p == 1)
        def _():
            for h in swapped:
                b_copy(1, h).start()

    inv_row = 1.0 / jnp.sqrt(sums[0:1] / total_width + EPSILON)
    if not paired:
        inv_out[...] = jnp.broadcast_to(inv_row, inv_out.shape)
        for d in range(1, layers):

            @pl.when(p >= d)
            def _():
                inv_copy(d).start()

    inv = to_col(inv_row)

    def wait_inv():
        for d in range(1, layers):

            @pl.when(p + d < layers)
            def _():
                inv_copy(d).wait_recv()

    def wait_b(some):
        for d in range(1, layers):

            @pl.when(p + d < layers)
            def _():
                for h in some:
                    b_copy(d, h).wait_recv()

    def later(h, later_inv):
        incoming = top[:, cols(h)].astype(F32)
        for d in range(1, layers):
            incoming = incoming * (1.0 + b_in[d - 1, h].astype(F32) * later_inv[d - 1])
        return incoming

    if merged:
        mean_row = sums[1:2]
        later_inv = []
        if paired:

            @pl.when(p == 0)
            def _():
                seconds = jnp.zeros((rows, LANES), F32)
                for h in order:
                    if h not in swapped:
                        wait_b([h])
                        seconds = seconds + ng[:, cols(h)] * att[:, cols(h)] * b_in[0, h].astype(F32)
                row_start(1, (seconds,))
                mix_all().wait_recv()
                total = mix_in[0]
                for e in range(1, shards):
                    total = total + mix_in[e]
                above = 1.0 / jnp.sqrt(total[0:1] / total_width + EPSILON)
                inv_in[0] = jnp.broadcast_to(above, inv_in.shape[1:])
                inv_out[...] = jnp.broadcast_to(total[1:2], inv_out.shape)

            later_inv = [to_col(inv_in[0])]
        for h in order:
            if h not in swapped:
                scaled = ng[:, cols(h)] * inv
                if paired:
                    scaled = scaled * (1.0 + b_in[0, h].astype(F32) * later_inv[0])
                ng[:, cols(h)] = scaled
        if paired:

            @pl.when(p == 0)
            def _():
                total = row_finish(1)
                row_sent(1)
                rows_out[1] = jnp.broadcast_to(total[0:1] + inv_out[0:1], rows_out.shape[1:])

            @pl.when(p == 1)
            def _():
                rows_out[1] = jnp.zeros(rows_out.shape[1:], F32)

            mean_row = mean_row + inv_in[0, 0:1] * rows_out[1, 0:1]
        mean_row = mean_row * inv_row
    else:
        wait_inv()
        later_inv = [to_col(inv_in[d - 1]) for d in range(1, layers)]
        products = jnp.zeros((rows, LANES), F32)
        for h in range(heads):
            wait_b([h])
            weighted = later(h, later_inv) * (gain[:, cols(h)] * gate[:, cols(h)])
            ng[:, cols(h)] = weighted
            products = products + weighted * att[:, cols(h)] * inv
        row_start(1, (products,))
        mean_row = row_finish(1)
    scale = to_col(mean_row / total_width * inv_row * inv_row)
    for h in order:
        scaled = ng[:, cols(h)]
        if not merged:
            scaled = scaled * inv
        if h in swapped:
            wait_b([h])
            scaled = scaled * inv * (1.0 + b_in[0, h].astype(F32) * later_inv[0])
        grad = (scaled - att[:, cols(h)] * scale).astype(BF16)
        ag[:, cols(h)] = grad
        states[h] = dot(q[:, cols(h)], grad, 0, 0)
        if blocks > 1:

            @pl.when(c == blocks - 1)
            def _():
                first(suf_copy, suf_out, h)

    def inner_grads(h):
        sig = gate[:, cols(h)]
        slope = gain[:, cols(h)] * sig * (1.0 - sig)
        factor = 1.0 + att[:, cols(h)] * inv * slope
        sec[:, cols(h)] = (later(h, later_inv) * factor).astype(BF16)
        query, key, value = q[:, cols(h)], k[:, cols(h)], v[:, cols(h)]
        grad = ag[:, cols(h)]
        score_grad = jnp.where(causal, dot(grad, value, 1, 1), 0.0).astype(BF16)
        query_grad = dot(score_grad, key, 1, 0) + dot(grad, pre_in[h], 1, 1)
        qg[:, cols(h)] = query_grad.astype(BF16)
        att[:, cols(h)] = dot(score_grad, query, 0, 0)
        ng[:, cols(h)] = dot(scores[h], grad, 0, 0)

    trail = max(heads - TRAIL, 0) if blocks > 1 else heads
    for h in order[:trail]:
        inner_grads(h)
    if trail < heads:

        @pl.when(c != blocks - 2)
        def _():
            for h in order[trail:]:
                inner_grads(h)

    for place, h in enumerate(order):
        if blocks > 1:
            forward(suf_copy, suf_in, suf_out, h, (c < blocks - 1) & (c > 0), (c < blocks - 1) & (c == 0))
        if trail + place < heads:

            @pl.when(c == blocks - 2)
            def _():
                inner_grads(order[trail + place])

        suffix = suf_in[h]
        key_grad = att[:, cols(h)] + dot(v[:, cols(h)], suffix, 1, 1)
        kg[:, cols(h)] = key_grad.astype(BF16)
        value_grad = ng[:, cols(h)] + dot(k[:, cols(h)], suffix, 1, 0)
        vg[:, cols(h)] = value_grad.astype(BF16)

    if blocks > 1:

        @pl.when(c < blocks - 1)
        def _():
            pltpu.make_async_remote_copy(
                src_ref=pre_out, dst_ref=pre_in,
                send_sem=chain_send.at[0], recv_sem=chain_recv.at[0, 0],
                device_id={"cp": c + 1}, device_id_type=MESH,
            ).wait_send()

        @pl.when(c > 0)
        def _():
            pltpu.make_async_remote_copy(
                src_ref=suf_out, dst_ref=suf_in,
                send_sem=chain_send.at[1], recv_sem=chain_recv.at[0, 0],
                device_id={"cp": c - 1}, device_id_type=MESH,
            ).wait_send()

    for d in range(1, layers):

        @pl.when(p >= d)
        def _():
            if paired:
                mix_all().wait_send()
            else:
                inv_copy(d).wait_send()
            pltpu.make_async_remote_copy(
                src_ref=b_out, dst_ref=b_in.at[d - 1],
                send_sem=b_send.at[d - 1], recv_sem=b_recv.at[d - 1, 0],
                device_id={"pp": p - d}, device_id_type=MESH,
            ).wait_send()

    if swapped:

        @pl.when(p == 0)
        def _():
            z_all().wait_send()

    row_sent(0)
    if not merged:
        row_sent(1)


def write_kernel(outs, sec_hbm, qg_hbm, kg_hbm, vg_hbm, sem):
    rows = outs.shape[1]
    step = rows // 4 if rows % 32 == 0 else rows
    dsts = (sec_hbm, qg_hbm, kg_hbm, vg_hbm)
    for i, dst in enumerate(dsts):
        for r in range(0, rows, step):
            pltpu.make_async_copy(
                outs.at[i, r : r + step], dst.at[0, r : r + step], sem.at[i]
            ).start()
    for i, dst in enumerate(dsts):
        pltpu.make_async_copy(outs.at[i], dst.at[0], sem.at[i]).wait()


def on_device(sizes, q, k, v, x, top, gains):
    layers, blocks, shards = sizes
    rows, width = q.shape[1:]
    heads = width // HEAD
    padded = -(-rows // LANES) * LANES
    others, peers = max(layers - 1, 1), max(shards - 1, 1)
    swaps = max(len(swapped_heads(heads)), 1)
    wide = pltpu.VMEM((rows, width), BF16)
    wide32 = pltpu.VMEM((rows, width), F32)
    square = pltpu.VMEM((heads, HEAD, HEAD), BF16)
    dma = pltpu.SemaphoreType.DMA
    out = jax.ShapeDtypeStruct((1, rows, width), BF16)
    q, k, v, x, top, gains = (
        pltpu.with_memory_space_constraint(a, pltpu.HBM) for a in (q, k, v, x, top, gains)
    )
    outs = pl.pallas_call(
        functools.partial(kernel, sizes),
        out_shape=jax.ShapeDtypeStruct((4, rows, width), BF16),
        in_specs=[pl.BlockSpec(memory_space=pltpu.HBM)] * 6,
        out_specs=pl.BlockSpec(memory_space=pltpu.VMEM),
        scratch_shapes=[
            wide, wide, wide, wide, wide, pltpu.VMEM((1, width), F32),
            square, square, square, square,
            pltpu.VMEM((heads, HEAD, HEAD), F32),
            pltpu.VMEM((heads, rows, rows), BF16),
            wide32, wide32, wide32, wide,
            pltpu.VMEM((heads, rows, HEAD), BF16),
            pltpu.VMEM((others, heads, rows, HEAD), BF16),
            pltpu.VMEM((2, 8, padded), F32),
            pltpu.VMEM((2, peers, 8, padded), F32),
            pltpu.VMEM((8, padded), F32),
            pltpu.VMEM((others, 8, padded), F32),
            pltpu.VMEM((swaps, rows, HEAD), BF16),
            pltpu.VMEM((swaps, rows, HEAD), BF16),
            pltpu.VMEM((8, padded), F32),
            pltpu.VMEM((shards, 8, padded), F32),
            dma((6,)),
            dma((2,)), dma((heads, PIECES)),
            dma((others,)), dma((others, heads)),
            dma((2,)), dma((2,)),
            dma((others,)), dma((others,)),
            dma((2,)), dma((2,)),
        ],
        compiler_params=pltpu.CompilerParams(collective_id=0, has_side_effects=True, vmem_limit_bytes=VMEM_LIMIT),
    )(q, k, v, x, top, gains)
    return pl.pallas_call(
        write_kernel,
        out_shape=(out,) * 4,
        in_specs=[pl.BlockSpec(memory_space=pltpu.VMEM)],
        out_specs=(pl.BlockSpec(memory_space=pl.ANY),) * 4,
        scratch_shapes=[dma((4,))],
        compiler_params=pltpu.CompilerParams(vmem_limit_bytes=1 << 20),
    )(outs)


def solution(mesh):
    sizes = (mesh.shape["pp"], mesh.shape["cp"], mesh.shape["tp"])
    part = P("pp", "cp", "tp")
    return jax.shard_map(
        functools.partial(on_device, sizes),
        mesh=mesh,
        in_specs=(part, part, part, part, P("cp", "tp"), P("pp", "tp")),
        out_specs=(part, part, part, part),
        check_vma=False,
    )
```

```python
import functools

import jax
import jax.numpy as jnp
from jax import lax
from jax.experimental import pallas as pl
from jax.experimental.pallas import tpu as pltpu
from jax.sharding import PartitionSpec as P

HEAD = 128
LANES = 128
EPSILON = 1e-06
PIECES = 4
LEAD = 2
TRAIL = 2
SWAPPED = (3, 5, 6)
PACKED = 2
VMEM_LIMIT = 24 << 20
MESH = pl.DeviceIdType.MESH
F32 = jnp.float32
BF16 = jnp.bfloat16


def dot(a, b, a_dim, b_dim):
    return lax.dot_general(a, b, (((a_dim,), (b_dim,)), ((), ())), preferred_element_type=F32)


def swapped_heads(heads):
    return [h for h in SWAPPED if h < heads]


def kernel(
    sizes,
    q_hbm, k_hbm, v_hbm, x_hbm, top_hbm, gain_hbm,
    outs,
    q, k, v, x, top, gain,
    pre_in, pre_out, suf_in, suf_out, states, scores, att, ng, gate, ag, b_out, b_in,
    rows_out, rows_in, inv_out, inv_in, z_out, z_in, mix_out, mix_in,
    in_sem, chain_send, chain_recv,
    b_send, b_recv, row_send, row_recv, inv_send, inv_recv, mix_sem, z_sem,
):
    layers, blocks, shards = sizes
    p = lax.axis_index("pp") if layers > 1 else jnp.int32(0)
    c = lax.axis_index("cp") if blocks > 1 else jnp.int32(0)
    t = lax.axis_index("tp") if shards > 1 else jnp.int32(0)
    rows, width = q.shape
    sec, qg, kg, vg = (outs.at[i] for i in range(4))
    heads = width // HEAD
    padded = rows_out.shape[2]
    swapped = swapped_heads(heads) if layers == 2 else []
    paired = len(swapped) > 0
    order = [h for h in range(heads) if h not in swapped] + swapped
    total_width = width * shards

    def part(i):
        return slice(i * (HEAD // PIECES), (i + 1) * (HEAD // PIECES))

    def cols(h):
        return slice(h * HEAD, (h + 1) * HEAD)

    loads = [
        pltpu.make_async_copy(k_hbm.at[0], k, in_sem.at[0]),
        pltpu.make_async_copy(v_hbm.at[0], v, in_sem.at[1]),
        pltpu.make_async_copy(q_hbm.at[0], q, in_sem.at[2]),
        pltpu.make_async_copy(x_hbm.at[0], x, in_sem.at[3]),
        pltpu.make_async_copy(gain_hbm, gain, in_sem.at[4]),
        pltpu.make_async_copy(top_hbm, top, in_sem.at[5]),
    ]
    for load in loads[:2]:
        load.start()

    barrier = pltpu.get_barrier_semaphore()

    @pl.when(c > 0)
    def _():
        pl.semaphore_signal(barrier, inc=1, device_id={"cp": c - 1}, device_id_type=MESH)

    @pl.when(c < blocks - 1)
    def _():
        pl.semaphore_signal(barrier, inc=1, device_id={"cp": c + 1}, device_id_type=MESH)

    for d in range(1, shards):
        pl.semaphore_signal(
            barrier, inc=1, device_id={"tp": lax.rem(t + d, shards)}, device_id_type=MESH
        )
    for d in range(1, layers):
        pl.semaphore_signal(
            barrier, inc=1, device_id={"pp": lax.rem(p + d, layers)}, device_id_type=MESH
        )

    @pl.when(c == 0)
    def _():
        pre_in[...] = jnp.zeros_like(pre_in)

    @pl.when(c == blocks - 1)
    def _():
        suf_in[...] = jnp.zeros_like(suf_in)

    for d in range(1, layers):

        @pl.when(p + d >= layers)
        def _():
            b_in[d - 1] = jnp.zeros(b_in.shape[1:], b_in.dtype)
            inv_in[d - 1] = jnp.zeros(inv_in.shape[1:], inv_in.dtype)

    def pre_copy(h, i):
        return pltpu.make_async_remote_copy(
            src_ref=pre_out.at[h, part(i)], dst_ref=pre_in.at[h, part(i)],
            send_sem=chain_send.at[0], recv_sem=chain_recv.at[h, i],
            device_id={"cp": c + 1}, device_id_type=MESH,
        )

    def suf_copy(h, i):
        return pltpu.make_async_remote_copy(
            src_ref=suf_out.at[h, part(i)], dst_ref=suf_in.at[h, part(i)],
            send_sem=chain_send.at[1], recv_sem=chain_recv.at[h, i],
            device_id={"cp": c - 1}, device_id_type=MESH,
        )

    def b_copy(d, h):
        return pltpu.make_async_remote_copy(
            src_ref=b_out.at[h], dst_ref=b_in.at[d - 1, h],
            send_sem=b_send.at[d - 1], recv_sem=b_recv.at[d - 1, h],
            device_id={"pp": p - d}, device_id_type=MESH,
        )

    def inv_copy(d):
        return pltpu.make_async_remote_copy(
            src_ref=inv_out, dst_ref=inv_in.at[d - 1],
            send_sem=inv_send.at[d - 1], recv_sem=inv_recv.at[d - 1],
            device_id={"pp": p - d}, device_id_type=MESH,
        )

    def z_copy(j):
        return pltpu.make_async_remote_copy(
            src_ref=z_out.at[j], dst_ref=z_in.at[j],
            send_sem=z_sem.at[0], recv_sem=z_sem.at[1],
            device_id={"pp": p + 1}, device_id_type=MESH,
        )

    def z_all():
        return pltpu.make_async_remote_copy(
            src_ref=z_out, dst_ref=z_in,
            send_sem=z_sem.at[0], recv_sem=z_sem.at[1],
            device_id={"pp": p + 1}, device_id_type=MESH,
        )

    def mix_copy(e):
        return pltpu.make_async_remote_copy(
            src_ref=mix_out, dst_ref=mix_in.at[e],
            send_sem=mix_sem.at[0], recv_sem=mix_sem.at[1],
            device_id={"pp": p - 1, "tp": lax.rem(t + e, shards)}, device_id_type=MESH,
        )

    def mix_all():
        return pltpu.make_async_remote_copy(
            src_ref=mix_in, dst_ref=mix_in,
            send_sem=mix_sem.at[0], recv_sem=mix_sem.at[1],
            device_id={"pp": p - 1}, device_id_type=MESH,
        )

    def row_copy(i, d):
        return pltpu.make_async_remote_copy(
            src_ref=rows_out.at[i], dst_ref=rows_in.at[i, d - 1],
            send_sem=row_send.at[i], recv_sem=row_recv.at[i],
            device_id={"tp": lax.rem(t + d, shards)}, device_id_type=MESH,
        )

    def to_row(partial):
        if padded > rows:
            fill = jnp.zeros((padded - rows, LANES), F32)
            partial = jnp.concatenate([partial, fill], axis=0)
        return jnp.broadcast_to(jnp.sum(partial.T, axis=0, keepdims=True), (PACKED, padded))

    def to_col(row):
        return jnp.broadcast_to(row[0:1], (LANES, padded)).T[:rows]

    def row_start(i, partials):
        ids = lax.broadcasted_iota(jnp.int32, (PACKED, padded), 0)
        packed = to_row(partials[0])
        for j in range(1, len(partials)):
            packed = jnp.where(ids == j, to_row(partials[j]), packed)
        rows_out[i] = packed
        for d in range(1, shards):
            row_copy(i, d).start()

    def row_all(i):
        return pltpu.make_async_remote_copy(
            src_ref=rows_in.at[i], dst_ref=rows_in.at[i],
            send_sem=row_send.at[i], recv_sem=row_recv.at[i],
            device_id={"tp": lax.rem(t + 1, shards)}, device_id_type=MESH,
        )

    def row_finish(i):
        total = rows_out[i]
        if shards > 1:
            row_all(i).wait_recv()
        for d in range(1, shards):
            total = total + rows_in[i, d - 1]
        return total

    def row_sent(i):
        if shards > 1:
            row_all(i).wait_send()

    causal = lax.broadcasted_iota(jnp.int32, (rows, rows), 0) >= lax.broadcasted_iota(
        jnp.int32, (rows, rows), 1
    )

    def forward(copy, arrived, sent, h, inner, outer):
        @pl.when(inner)
        def _():
            for i in range(PIECES):
                copy(h, i).wait_recv()
                total = arrived[h, part(i)].astype(F32) + states[h, part(i)]
                sent[h, part(i)] = total.astype(BF16)
                copy(h, i).start()

        @pl.when(outer)
        def _():
            for i in range(PIECES):
                copy(h, i).wait_recv()

    def first(copy, sent, h):
        for i in range(PIECES):
            sent[h, part(i)] = states[h, part(i)].astype(BF16)
            copy(h, i).start()

    def local(h):
        query, value = q[:, cols(h)], v[:, cols(h)]
        score = jnp.where(causal, dot(query, k[:, cols(h)], 1, 1), 0.0).astype(BF16)
        scores[h] = score
        att[:, cols(h)] = dot(score, value, 1, 0)
        gate[:, cols(h)] = jax.nn.sigmoid(x[:, cols(h)].astype(F32))

    loads[0].wait()
    loads[1].wait()
    for load in loads[2:]:
        load.start()
    states[0] = dot(k[:, cols(0)], v[:, cols(0)], 0, 0)
    partners = (shards - 1) + (layers - 1)
    pl.semaphore_wait(
        barrier, partners + jnp.where(c > 0, 1, 0) + jnp.where(c < blocks - 1, 1, 0)
    )
    for h in range(heads):
        if h > 0:
            states[h] = dot(k[:, cols(h)], v[:, cols(h)], 0, 0)
        if blocks > 1:

            @pl.when(c == 0)
            def _():
                first(pre_copy, pre_out, h)

    for load in loads[2:]:
        load.wait()
    lead = min(LEAD, heads) if blocks > 1 else heads
    for h in range(lead):
        local(h)
    if lead < heads:

        @pl.when(c != 1)
        def _():
            for h in range(lead, heads):
                local(h)

    merged = layers == 1 or paired
    squares = jnp.zeros((rows, LANES), F32)
    firsts = jnp.zeros((rows, LANES), F32)
    for h in range(heads):
        if blocks > 1:
            forward(pre_copy, pre_in, pre_out, h, (c > 0) & (c < blocks - 1), (c > 0) & (c == blocks - 1))
        attention = att[:, cols(h)] + dot(q[:, cols(h)], pre_in[h], 1, 0)
        att[:, cols(h)] = attention
        squares = squares + attention * attention
        sig = gate[:, cols(h)]
        if merged:
            weighted = top[:, cols(h)].astype(F32) * (gain[:, cols(h)] * sig)
            ng[:, cols(h)] = weighted
            firsts = firsts + weighted * attention
        if layers > 1:
            b_out[h] = (attention * (gain[:, cols(h)] * sig * (1.0 - sig))).astype(BF16)
        if h in swapped:

            @pl.when(p == 0)
            def _():
                z_out[swapped.index(h)] = (weighted * attention).astype(BF16)
                z_copy(swapped.index(h)).start()

        else:
            for d in range(1, layers):

                @pl.when(p >= d)
                def _():
                    b_copy(d, h).start()

        if h + lead < heads:

            @pl.when(c == 1)
            def _():
                local(h + lead)

    row_start(0, (squares, firsts))
    if paired:

        @pl.when(p == 1)
        def _():
            seconds = jnp.zeros((rows, LANES), F32)
            z_all().wait_recv()
            for j, h in enumerate(swapped):
                seconds = seconds + z_in[j].astype(F32) * b_out[h].astype(F32)
            ids = lax.broadcasted_iota(jnp.int32, (PACKED, padded), 0)
            mix_out[...] = jnp.where(ids == 1, to_row(seconds), rows_out[0])
            for e in range(shards):
                mix_copy(e).start()

    sums = row_finish(0)
    if paired:

        @pl.when(p == 1)
        def _():
            for h in swapped:
                b_copy(1, h).start()

    inv_row = 1.0 / jnp.sqrt(sums[0:1] / total_width + EPSILON)
    if not paired:
        inv_out[...] = jnp.broadcast_to(inv_row, inv_out.shape)
        for d in range(1, layers):

            @pl.when(p >= d)
            def _():
                inv_copy(d).start()

    inv = to_col(inv_row)

    def wait_inv():
        for d in range(1, layers):

            @pl.when(p + d < layers)
            def _():
                inv_copy(d).wait_recv()

    def wait_b(some):
        for d in range(1, layers):

            @pl.when(p + d < layers)
            def _():
                for h in some:
                    b_copy(d, h).wait_recv()

    def later(h, later_inv):
        incoming = top[:, cols(h)].astype(F32)
        for d in range(1, layers):
            incoming = incoming * (1.0 + b_in[d - 1, h].astype(F32) * later_inv[d - 1])
        return incoming

    if merged:
        mean_row = sums[1:2]
        later_inv = []
        if paired:

            @pl.when(p == 0)
            def _():
                seconds = jnp.zeros((rows, LANES), F32)
                for h in order:
                    if h not in swapped:
                        wait_b([h])
                        seconds = seconds + ng[:, cols(h)] * att[:, cols(h)] * b_in[0, h].astype(F32)
                row_start(1, (seconds,))
                mix_all().wait_recv()
                total = mix_in[0]
                for e in range(1, shards):
                    total = total + mix_in[e]
                above = 1.0 / jnp.sqrt(total[0:1] / total_width + EPSILON)
                inv_in[0] = jnp.broadcast_to(above, inv_in.shape[1:])
                inv_out[...] = jnp.broadcast_to(total[1:2], inv_out.shape)

            later_inv = [to_col(inv_in[0])]
        for h in order:
            if h not in swapped:
                scaled = ng[:, cols(h)] * inv
                if paired:
                    scaled = scaled * (1.0 + b_in[0, h].astype(F32) * later_inv[0])
                ng[:, cols(h)] = scaled
        if paired:

            @pl.when(p == 0)
            def _():
                total = row_finish(1)
                row_sent(1)
                rows_out[1] = jnp.broadcast_to(total[0:1] + inv_out[0:1], rows_out.shape[1:])

            @pl.when(p == 1)
            def _():
                rows_out[1] = jnp.zeros(rows_out.shape[1:], F32)

            mean_row = mean_row + inv_in[0, 0:1] * rows_out[1, 0:1]
        mean_row = mean_row * inv_row
    else:
        wait_inv()
        later_inv = [to_col(inv_in[d - 1]) for d in range(1, layers)]
        products = jnp.zeros((rows, LANES), F32)
        for h in range(heads):
            wait_b([h])
            weighted = later(h, later_inv) * (gain[:, cols(h)] * gate[:, cols(h)])
            ng[:, cols(h)] = weighted
            products = products + weighted * att[:, cols(h)] * inv
        row_start(1, (products,))
        mean_row = row_finish(1)
    scale = to_col(mean_row / total_width * inv_row * inv_row)
    for h in order:
        scaled = ng[:, cols(h)]
        if not merged:
            scaled = scaled * inv
        if h in swapped:
            wait_b([h])
            scaled = scaled * inv * (1.0 + b_in[0, h].astype(F32) * later_inv[0])
        grad = (scaled - att[:, cols(h)] * scale).astype(BF16)
        ag[:, cols(h)] = grad
        states[h] = dot(q[:, cols(h)], grad, 0, 0)
        if blocks > 1:

            @pl.when(c == blocks - 1)
            def _():
                first(suf_copy, suf_out, h)

    def inner_grads(h):
        sig = gate[:, cols(h)]
        slope = gain[:, cols(h)] * sig * (1.0 - sig)
        factor = 1.0 + att[:, cols(h)] * inv * slope
        sec[:, cols(h)] = (later(h, later_inv) * factor).astype(BF16)
        query, key, value = q[:, cols(h)], k[:, cols(h)], v[:, cols(h)]
        grad = ag[:, cols(h)]
        score_grad = jnp.where(causal, dot(grad, value, 1, 1), 0.0).astype(BF16)
        query_grad = dot(score_grad, key, 1, 0) + dot(grad, pre_in[h], 1, 1)
        qg[:, cols(h)] = query_grad.astype(BF16)
        att[:, cols(h)] = dot(score_grad, query, 0, 0)
        ng[:, cols(h)] = dot(scores[h], grad, 0, 0)

    trail = max(heads - TRAIL, 0) if blocks > 1 else heads
    for h in order[:trail]:
        inner_grads(h)
    if trail < heads:

        @pl.when(c != blocks - 2)
        def _():
            for h in order[trail:]:
                inner_grads(h)

    for place, h in enumerate(order):
        if blocks > 1:
            forward(suf_copy, suf_in, suf_out, h, (c < blocks - 1) & (c > 0), (c < blocks - 1) & (c == 0))
        if trail + place < heads:

            @pl.when(c == blocks - 2)
            def _():
                inner_grads(order[trail + place])

        suffix = suf_in[h]
        key_grad = att[:, cols(h)] + dot(v[:, cols(h)], suffix, 1, 1)
        kg[:, cols(h)] = key_grad.astype(BF16)
        value_grad = ng[:, cols(h)] + dot(k[:, cols(h)], suffix, 1, 0)
        vg[:, cols(h)] = value_grad.astype(BF16)

    if blocks > 1:

        @pl.when(c < blocks - 1)
        def _():
            pltpu.make_async_remote_copy(
                src_ref=pre_out, dst_ref=pre_in,
                send_sem=chain_send.at[0], recv_sem=chain_recv.at[0, 0],
                device_id={"cp": c + 1}, device_id_type=MESH,
            ).wait_send()

        @pl.when(c > 0)
        def _():
            pltpu.make_async_remote_copy(
                src_ref=suf_out, dst_ref=suf_in,
                send_sem=chain_send.at[1], recv_sem=chain_recv.at[0, 0],
                device_id={"cp": c - 1}, device_id_type=MESH,
            ).wait_send()

    for d in range(1, layers):

        @pl.when(p >= d)
        def _():
            if paired:
                mix_all().wait_send()
            else:
                inv_copy(d).wait_send()
            pltpu.make_async_remote_copy(
                src_ref=b_out, dst_ref=b_in.at[d - 1],
                send_sem=b_send.at[d - 1], recv_sem=b_recv.at[d - 1, 0],
                device_id={"pp": p - d}, device_id_type=MESH,
            ).wait_send()

    if swapped:

        @pl.when(p == 0)
        def _():
            z_all().wait_send()

    row_sent(0)
    if not merged:
        row_sent(1)


def write_kernel(outs, sec_hbm, qg_hbm, kg_hbm, vg_hbm, sem):
    rows = outs.shape[1]
    step = rows // 4 if rows % 32 == 0 else rows
    dsts = (sec_hbm, qg_hbm, kg_hbm, vg_hbm)
    for i, dst in enumerate(dsts):
        for r in range(0, rows, step):
            pltpu.make_async_copy(
                outs.at[i, r : r + step], dst.at[0, r : r + step], sem.at[i]
            ).start()
    for i, dst in enumerate(dsts):
        pltpu.make_async_copy(outs.at[i], dst.at[0], sem.at[i]).wait()


def on_device(sizes, q, k, v, x, top, gains):
    layers, blocks, shards = sizes
    rows, width = q.shape[1:]
    heads = width // HEAD
    padded = -(-rows // LANES) * LANES
    others, peers = max(layers - 1, 1), max(shards - 1, 1)
    swaps = max(len(swapped_heads(heads)), 1)
    wide = pltpu.VMEM((rows, width), BF16)
    wide32 = pltpu.VMEM((rows, width), F32)
    square = pltpu.VMEM((heads, HEAD, HEAD), BF16)
    dma = pltpu.SemaphoreType.DMA
    out = jax.ShapeDtypeStruct((1, rows, width), BF16)
    q, k, v, x, top, gains = (
        pltpu.with_memory_space_constraint(a, pltpu.HBM) for a in (q, k, v, x, top, gains)
    )
    outs = pl.pallas_call(
        functools.partial(kernel, sizes),
        out_shape=jax.ShapeDtypeStruct((4, rows, width), BF16),
        in_specs=[pl.BlockSpec(memory_space=pltpu.HBM)] * 6,
        out_specs=pl.BlockSpec(memory_space=pltpu.VMEM),
        scratch_shapes=[
            wide, wide, wide, wide, wide, pltpu.VMEM((1, width), F32),
            square, square, square, square,
            pltpu.VMEM((heads, HEAD, HEAD), F32),
            pltpu.VMEM((heads, rows, rows), BF16),
            wide32, wide32, wide32, wide,
            pltpu.VMEM((heads, rows, HEAD), BF16),
            pltpu.VMEM((others, heads, rows, HEAD), BF16),
            pltpu.VMEM((2, PACKED, padded), F32),
            pltpu.VMEM((2, peers, PACKED, padded), F32),
            pltpu.VMEM((8, padded), F32),
            pltpu.VMEM((others, 8, padded), F32),
            pltpu.VMEM((swaps, rows, HEAD), BF16),
            pltpu.VMEM((swaps, rows, HEAD), BF16),
            pltpu.VMEM((PACKED, padded), F32),
            pltpu.VMEM((shards, PACKED, padded), F32),
            dma((6,)),
            dma((2,)), dma((heads, PIECES)),
            dma((others,)), dma((others, heads)),
            dma((2,)), dma((2,)),
            dma((others,)), dma((others,)),
            dma((2,)), dma((2,)),
        ],
        compiler_params=pltpu.CompilerParams(collective_id=0, has_side_effects=True, vmem_limit_bytes=VMEM_LIMIT),
    )(q, k, v, x, top, gains)
    return pl.pallas_call(
        write_kernel,
        out_shape=(out,) * 4,
        in_specs=[pl.BlockSpec(memory_space=pltpu.VMEM)],
        out_specs=(pl.BlockSpec(memory_space=pl.ANY),) * 4,
        scratch_shapes=[dma((4,))],
        compiler_params=pltpu.CompilerParams(vmem_limit_bytes=1 << 20),
    )(outs)


def solution(mesh):
    sizes = (mesh.shape["pp"], mesh.shape["cp"], mesh.shape["tp"])
    part = P("pp", "cp", "tp")
    return jax.shard_map(
        functools.partial(on_device, sizes),
        mesh=mesh,
        in_specs=(part, part, part, part, P("cp", "tp"), P("pp", "tp")),
        out_specs=(part, part, part, part),
        check_vma=False,
    )
```

```python
import functools

import jax
import jax.numpy as jnp
from jax import lax
from jax.experimental import pallas as pl
from jax.experimental.pallas import tpu as pltpu
from jax.sharding import PartitionSpec as P

HEAD = 128
LANES = 128
EPSILON = 1e-06
PIECES = 4
LEAD = 2
SWAPPED = (3, 5, 6)
PACKED = 2
VMEM_LIMIT = 24 << 20
MESH = pl.DeviceIdType.MESH
F32 = jnp.float32
BF16 = jnp.bfloat16


def dot(a, b, a_dim, b_dim):
    return lax.dot_general(a, b, (((a_dim,), (b_dim,)), ((), ())), preferred_element_type=F32)


def swapped_heads(heads):
    return [h for h in SWAPPED if h < heads]


def kernel(
    sizes,
    q_hbm, k_hbm, v_hbm, x_hbm, top_hbm, gain_hbm,
    outs,
    q, k, v, x, top, gain,
    pre_in, pre_out, suf_in, suf_out, states, scores, att, ng, gate, ag, b_out, b_in,
    rows_out, rows_in, inv_out, inv_in, z_out, z_in, mix_out, mix_in,
    in_sem, chain_send, chain_recv,
    b_send, b_recv, row_send, row_recv, inv_send, inv_recv, mix_sem, z_sem,
):
    layers, blocks, shards = sizes
    p = lax.axis_index("pp") if layers > 1 else jnp.int32(0)
    c = lax.axis_index("cp") if blocks > 1 else jnp.int32(0)
    t = lax.axis_index("tp") if shards > 1 else jnp.int32(0)
    rows, width = q.shape
    sec, qg, kg, vg = (outs.at[i] for i in range(4))
    heads = width // HEAD
    padded = rows_out.shape[2]
    swapped = swapped_heads(heads) if layers == 2 else []
    paired = len(swapped) > 0
    order = [h for h in range(heads) if h not in swapped] + swapped
    total_width = width * shards

    def part(i):
        return slice(i * (HEAD // PIECES), (i + 1) * (HEAD // PIECES))

    def cols(h):
        return slice(h * HEAD, (h + 1) * HEAD)

    loads = [
        pltpu.make_async_copy(k_hbm.at[0], k, in_sem.at[0]),
        pltpu.make_async_copy(v_hbm.at[0], v, in_sem.at[1]),
        pltpu.make_async_copy(q_hbm.at[0], q, in_sem.at[2]),
        pltpu.make_async_copy(x_hbm.at[0], x, in_sem.at[3]),
        pltpu.make_async_copy(gain_hbm, gain, in_sem.at[4]),
        pltpu.make_async_copy(top_hbm, top, in_sem.at[5]),
    ]
    for load in loads[:2]:
        load.start()

    barrier = pltpu.get_barrier_semaphore()

    @pl.when(c > 0)
    def _():
        pl.semaphore_signal(barrier, inc=1, device_id={"cp": c - 1}, device_id_type=MESH)

    @pl.when(c < blocks - 1)
    def _():
        pl.semaphore_signal(barrier, inc=1, device_id={"cp": c + 1}, device_id_type=MESH)

    for d in range(1, shards):
        pl.semaphore_signal(
            barrier, inc=1, device_id={"tp": lax.rem(t + d, shards)}, device_id_type=MESH
        )
    for d in range(1, layers):
        pl.semaphore_signal(
            barrier, inc=1, device_id={"pp": lax.rem(p + d, layers)}, device_id_type=MESH
        )

    @pl.when(c == 0)
    def _():
        pre_in[...] = jnp.zeros_like(pre_in)

    @pl.when(c == blocks - 1)
    def _():
        suf_in[...] = jnp.zeros_like(suf_in)

    for d in range(1, layers):

        @pl.when(p + d >= layers)
        def _():
            b_in[d - 1] = jnp.zeros(b_in.shape[1:], b_in.dtype)
            inv_in[d - 1] = jnp.zeros(inv_in.shape[1:], inv_in.dtype)

    def pre_copy(h, i):
        return pltpu.make_async_remote_copy(
            src_ref=pre_out.at[h, part(i)], dst_ref=pre_in.at[h, part(i)],
            send_sem=chain_send.at[0], recv_sem=chain_recv.at[h, i],
            device_id={"cp": c + 1}, device_id_type=MESH,
        )

    def suf_copy(h, i):
        return pltpu.make_async_remote_copy(
            src_ref=suf_out.at[h, part(i)], dst_ref=suf_in.at[h, part(i)],
            send_sem=chain_send.at[1], recv_sem=chain_recv.at[h, i],
            device_id={"cp": c - 1}, device_id_type=MESH,
        )

    def b_copy(d, h):
        return pltpu.make_async_remote_copy(
            src_ref=b_out.at[h], dst_ref=b_in.at[d - 1, h],
            send_sem=b_send.at[d - 1], recv_sem=b_recv.at[d - 1, h],
            device_id={"pp": p - d}, device_id_type=MESH,
        )

    def inv_copy(d):
        return pltpu.make_async_remote_copy(
            src_ref=inv_out, dst_ref=inv_in.at[d - 1],
            send_sem=inv_send.at[d - 1], recv_sem=inv_recv.at[d - 1],
            device_id={"pp": p - d}, device_id_type=MESH,
        )

    def z_copy(j):
        return pltpu.make_async_remote_copy(
            src_ref=z_out.at[j], dst_ref=z_in.at[j],
            send_sem=z_sem.at[0], recv_sem=z_sem.at[1],
            device_id={"pp": p + 1}, device_id_type=MESH,
        )

    def z_all():
        return pltpu.make_async_remote_copy(
            src_ref=z_out, dst_ref=z_in,
            send_sem=z_sem.at[0], recv_sem=z_sem.at[1],
            device_id={"pp": p + 1}, device_id_type=MESH,
        )

    def mix_copy(e):
        return pltpu.make_async_remote_copy(
            src_ref=mix_out, dst_ref=mix_in.at[e],
            send_sem=mix_sem.at[0], recv_sem=mix_sem.at[1],
            device_id={"pp": p - 1, "tp": lax.rem(t + e, shards)}, device_id_type=MESH,
        )

    def mix_all():
        return pltpu.make_async_remote_copy(
            src_ref=mix_in, dst_ref=mix_in,
            send_sem=mix_sem.at[0], recv_sem=mix_sem.at[1],
            device_id={"pp": p - 1}, device_id_type=MESH,
        )

    def row_copy(i, d):
        return pltpu.make_async_remote_copy(
            src_ref=rows_out.at[i], dst_ref=rows_in.at[i, d - 1],
            send_sem=row_send.at[i], recv_sem=row_recv.at[i],
            device_id={"tp": lax.rem(t + d, shards)}, device_id_type=MESH,
        )

    def to_row(partial):
        if padded > rows:
            fill = jnp.zeros((padded - rows, LANES), F32)
            partial = jnp.concatenate([partial, fill], axis=0)
        return jnp.broadcast_to(jnp.sum(partial.T, axis=0, keepdims=True), (PACKED, padded))

    def to_col(row):
        return jnp.broadcast_to(row[0:1], (LANES, padded)).T[:rows]

    def row_start(i, partials):
        ids = lax.broadcasted_iota(jnp.int32, (PACKED, padded), 0)
        packed = to_row(partials[0])
        for j in range(1, len(partials)):
            packed = jnp.where(ids == j, to_row(partials[j]), packed)
        rows_out[i] = packed
        for d in range(1, shards):
            row_copy(i, d).start()

    def row_all(i):
        return pltpu.make_async_remote_copy(
            src_ref=rows_in.at[i], dst_ref=rows_in.at[i],
            send_sem=row_send.at[i], recv_sem=row_recv.at[i],
            device_id={"tp": lax.rem(t + 1, shards)}, device_id_type=MESH,
        )

    def row_finish(i):
        total = rows_out[i]
        if shards > 1:
            row_all(i).wait_recv()
        for d in range(1, shards):
            total = total + rows_in[i, d - 1]
        return total

    def row_sent(i):
        if shards > 1:
            row_all(i).wait_send()

    causal = lax.broadcasted_iota(jnp.int32, (rows, rows), 0) >= lax.broadcasted_iota(
        jnp.int32, (rows, rows), 1
    )

    def relay(copy, arrived, sent, h, inner):
        @pl.when(inner)
        def _():
            for i in range(PIECES):
                copy(h, i).wait_recv()
                total = arrived[h, part(i)].astype(F32) + states[h, part(i)]
                sent[h, part(i)] = total.astype(BF16)
                copy(h, i).start()

    def absorb(copy, h, outer):
        @pl.when(outer)
        def _():
            for i in range(PIECES):
                copy(h, i).wait_recv()

    def first(copy, sent, h):
        for i in range(PIECES):
            sent[h, part(i)] = states[h, part(i)].astype(BF16)
            copy(h, i).start()

    def local(h):
        query, value = q[:, cols(h)], v[:, cols(h)]
        score = jnp.where(causal, dot(query, k[:, cols(h)], 1, 1), 0.0).astype(BF16)
        scores[h] = score
        att[:, cols(h)] = dot(score, value, 1, 0)
        gate[:, cols(h)] = jax.nn.sigmoid(x[:, cols(h)].astype(F32))

    loads[0].wait()
    loads[1].wait()
    for load in loads[2:]:
        load.start()
    states[0] = dot(k[:, cols(0)], v[:, cols(0)], 0, 0)
    partners = (shards - 1) + (layers - 1)
    pl.semaphore_wait(
        barrier, partners + jnp.where(c > 0, 1, 0) + jnp.where(c < blocks - 1, 1, 0)
    )
    for h in range(heads):
        if h > 0:
            states[h] = dot(k[:, cols(h)], v[:, cols(h)], 0, 0)
        if blocks > 1:

            @pl.when(c == 0)
            def _():
                first(pre_copy, pre_out, h)

    for load in loads[2:]:
        load.wait()
    lead = min(LEAD, heads) if blocks > 1 else heads
    for h in range(lead):
        local(h)
    if lead < heads:

        @pl.when(c != 1)
        def _():
            for h in range(lead, heads):
                local(h)

    merged = layers == 1 or paired
    squares = jnp.zeros((rows, LANES), F32)
    firsts = jnp.zeros((rows, LANES), F32)
    for h in range(heads):
        if blocks > 1:
            relay(pre_copy, pre_in, pre_out, h, (c > 0) & (c < blocks - 1))
            absorb(pre_copy, h, (c > 0) & (c == blocks - 1))
        attention = att[:, cols(h)] + dot(q[:, cols(h)], pre_in[h], 1, 0)
        att[:, cols(h)] = attention
        squares = squares + attention * attention
        sig = gate[:, cols(h)]
        if merged:
            weighted = top[:, cols(h)].astype(F32) * (gain[:, cols(h)] * sig)
            ng[:, cols(h)] = weighted
            firsts = firsts + weighted * attention
        if layers > 1:
            b_out[h] = (attention * (gain[:, cols(h)] * sig * (1.0 - sig))).astype(BF16)
        if h in swapped:

            @pl.when(p == 0)
            def _():
                z_out[swapped.index(h)] = (weighted * attention).astype(BF16)
                z_copy(swapped.index(h)).start()

        else:
            for d in range(1, layers):

                @pl.when(p >= d)
                def _():
                    b_copy(d, h).start()

        if h + lead < heads:

            @pl.when(c == 1)
            def _():
                local(h + lead)

    row_start(0, (squares, firsts))
    if paired:

        @pl.when(p == 1)
        def _():
            seconds = jnp.zeros((rows, LANES), F32)
            z_all().wait_recv()
            for j, h in enumerate(swapped):
                seconds = seconds + z_in[j].astype(F32) * b_out[h].astype(F32)
            ids = lax.broadcasted_iota(jnp.int32, (PACKED, padded), 0)
            mix_out[...] = jnp.where(ids == 1, to_row(seconds), rows_out[0])
            for e in range(shards):
                mix_copy(e).start()

    sums = row_finish(0)
    if paired:

        @pl.when(p == 1)
        def _():
            for h in swapped:
                b_copy(1, h).start()

    inv_row = 1.0 / jnp.sqrt(sums[0:1] / total_width + EPSILON)
    if not paired:
        inv_out[...] = jnp.broadcast_to(inv_row, inv_out.shape)
        for d in range(1, layers):

            @pl.when(p >= d)
            def _():
                inv_copy(d).start()

    inv = to_col(inv_row)

    def wait_inv():
        for d in range(1, layers):

            @pl.when(p + d < layers)
            def _():
                inv_copy(d).wait_recv()

    def wait_b(some):
        for d in range(1, layers):

            @pl.when(p + d < layers)
            def _():
                for h in some:
                    b_copy(d, h).wait_recv()

    def later(h, later_inv):
        incoming = top[:, cols(h)].astype(F32)
        for d in range(1, layers):
            incoming = incoming * (1.0 + b_in[d - 1, h].astype(F32) * later_inv[d - 1])
        return incoming

    if merged:
        mean_row = sums[1:2]
        later_inv = []
        if paired:

            @pl.when(p == 0)
            def _():
                seconds = jnp.zeros((rows, LANES), F32)
                for h in order:
                    if h not in swapped:
                        wait_b([h])
                        seconds = seconds + ng[:, cols(h)] * att[:, cols(h)] * b_in[0, h].astype(F32)
                row_start(1, (seconds,))
                mix_all().wait_recv()
                total = mix_in[0]
                for e in range(1, shards):
                    total = total + mix_in[e]
                above = 1.0 / jnp.sqrt(total[0:1] / total_width + EPSILON)
                inv_in[0] = jnp.broadcast_to(above, inv_in.shape[1:])
                inv_out[...] = jnp.broadcast_to(total[1:2], inv_out.shape)

            later_inv = [to_col(inv_in[0])]
        for h in order:
            if h not in swapped:
                scaled = ng[:, cols(h)] * inv
                if paired:
                    scaled = scaled * (1.0 + b_in[0, h].astype(F32) * later_inv[0])
                ng[:, cols(h)] = scaled
        if paired:

            @pl.when(p == 0)
            def _():
                total = row_finish(1)
                row_sent(1)
                rows_out[1] = jnp.broadcast_to(total[0:1] + inv_out[0:1], rows_out.shape[1:])

            @pl.when(p == 1)
            def _():
                rows_out[1] = jnp.zeros(rows_out.shape[1:], F32)

            mean_row = mean_row + inv_in[0, 0:1] * rows_out[1, 0:1]
        mean_row = mean_row * inv_row
    else:
        wait_inv()
        later_inv = [to_col(inv_in[d - 1]) for d in range(1, layers)]
        products = jnp.zeros((rows, LANES), F32)
        for h in range(heads):
            wait_b([h])
            weighted = later(h, later_inv) * (gain[:, cols(h)] * gate[:, cols(h)])
            ng[:, cols(h)] = weighted
            products = products + weighted * att[:, cols(h)] * inv
        row_start(1, (products,))
        mean_row = row_finish(1)
    scale = to_col(mean_row / total_width * inv_row * inv_row)
    for h in order:
        scaled = ng[:, cols(h)]
        if not merged:
            scaled = scaled * inv
        if h in swapped:
            wait_b([h])
            scaled = scaled * inv * (1.0 + b_in[0, h].astype(F32) * later_inv[0])
        grad = (scaled - att[:, cols(h)] * scale).astype(BF16)
        ag[:, cols(h)] = grad
        states[h] = dot(q[:, cols(h)], grad, 0, 0)
        if blocks > 1:

            @pl.when(c == blocks - 1)
            def _():
                first(suf_copy, suf_out, h)

    def inner_grads(h):
        sig = gate[:, cols(h)]
        slope = gain[:, cols(h)] * sig * (1.0 - sig)
        factor = 1.0 + att[:, cols(h)] * inv * slope
        sec[:, cols(h)] = (later(h, later_inv) * factor).astype(BF16)
        query, key, value = q[:, cols(h)], k[:, cols(h)], v[:, cols(h)]
        grad = ag[:, cols(h)]
        score_grad = jnp.where(causal, dot(grad, value, 1, 1), 0.0).astype(BF16)
        query_grad = dot(score_grad, key, 1, 0) + dot(grad, pre_in[h], 1, 1)
        qg[:, cols(h)] = query_grad.astype(BF16)
        att[:, cols(h)] = dot(score_grad, query, 0, 0)
        ng[:, cols(h)] = dot(scores[h], grad, 0, 0)

    for h in order:
        inner_grads(h)
    for h in order:
        if blocks > 1:
            relay(suf_copy, suf_in, suf_out, h, (c < blocks - 1) & (c > 0))
    for h in order:
        if blocks > 1:
            absorb(suf_copy, h, (c < blocks - 1) & (c == 0))
        suffix = suf_in[h]
        key_grad = att[:, cols(h)] + dot(v[:, cols(h)], suffix, 1, 1)
        kg[:, cols(h)] = key_grad.astype(BF16)
        value_grad = ng[:, cols(h)] + dot(k[:, cols(h)], suffix, 1, 0)
        vg[:, cols(h)] = value_grad.astype(BF16)

    if blocks > 1:

        @pl.when(c < blocks - 1)
        def _():
            pltpu.make_async_remote_copy(
                src_ref=pre_out, dst_ref=pre_in,
                send_sem=chain_send.at[0], recv_sem=chain_recv.at[0, 0],
                device_id={"cp": c + 1}, device_id_type=MESH,
            ).wait_send()

        @pl.when(c > 0)
        def _():
            pltpu.make_async_remote_copy(
                src_ref=suf_out, dst_ref=suf_in,
                send_sem=chain_send.at[1], recv_sem=chain_recv.at[0, 0],
                device_id={"cp": c - 1}, device_id_type=MESH,
            ).wait_send()

    for d in range(1, layers):

        @pl.when(p >= d)
        def _():
            if paired:
                mix_all().wait_send()
            else:
                inv_copy(d).wait_send()
            pltpu.make_async_remote_copy(
                src_ref=b_out, dst_ref=b_in.at[d - 1],
                send_sem=b_send.at[d - 1], recv_sem=b_recv.at[d - 1, 0],
                device_id={"pp": p - d}, device_id_type=MESH,
            ).wait_send()

    if swapped:

        @pl.when(p == 0)
        def _():
            z_all().wait_send()

    row_sent(0)
    if not merged:
        row_sent(1)


def write_kernel(outs, sec_hbm, qg_hbm, kg_hbm, vg_hbm, sem):
    rows = outs.shape[1]
    step = rows // 4 if rows % 32 == 0 else rows
    dsts = (sec_hbm, qg_hbm, kg_hbm, vg_hbm)
    for i, dst in enumerate(dsts):
        for r in range(0, rows, step):
            pltpu.make_async_copy(
                outs.at[i, r : r + step], dst.at[0, r : r + step], sem.at[i]
            ).start()
    for i, dst in enumerate(dsts):
        pltpu.make_async_copy(outs.at[i], dst.at[0], sem.at[i]).wait()


def on_device(sizes, q, k, v, x, top, gains):
    layers, blocks, shards = sizes
    rows, width = q.shape[1:]
    heads = width // HEAD
    padded = -(-rows // LANES) * LANES
    others, peers = max(layers - 1, 1), max(shards - 1, 1)
    swaps = max(len(swapped_heads(heads)), 1)
    wide = pltpu.VMEM((rows, width), BF16)
    wide32 = pltpu.VMEM((rows, width), F32)
    square = pltpu.VMEM((heads, HEAD, HEAD), BF16)
    dma = pltpu.SemaphoreType.DMA
    out = jax.ShapeDtypeStruct((1, rows, width), BF16)
    q, k, v, x, top, gains = (
        pltpu.with_memory_space_constraint(a, pltpu.HBM) for a in (q, k, v, x, top, gains)
    )
    outs = pl.pallas_call(
        functools.partial(kernel, sizes),
        out_shape=jax.ShapeDtypeStruct((4, rows, width), BF16),
        in_specs=[pl.BlockSpec(memory_space=pltpu.HBM)] * 6,
        out_specs=pl.BlockSpec(memory_space=pltpu.VMEM),
        scratch_shapes=[
            wide, wide, wide, wide, wide, pltpu.VMEM((1, width), F32),
            square, square, square, square,
            pltpu.VMEM((heads, HEAD, HEAD), F32),
            pltpu.VMEM((heads, rows, rows), BF16),
            wide32, wide32, wide32, wide,
            pltpu.VMEM((heads, rows, HEAD), BF16),
            pltpu.VMEM((others, heads, rows, HEAD), BF16),
            pltpu.VMEM((2, PACKED, padded), F32),
            pltpu.VMEM((2, peers, PACKED, padded), F32),
            pltpu.VMEM((8, padded), F32),
            pltpu.VMEM((others, 8, padded), F32),
            pltpu.VMEM((swaps, rows, HEAD), BF16),
            pltpu.VMEM((swaps, rows, HEAD), BF16),
            pltpu.VMEM((PACKED, padded), F32),
            pltpu.VMEM((shards, PACKED, padded), F32),
            dma((6,)),
            dma((2,)), dma((heads, PIECES)),
            dma((others,)), dma((others, heads)),
            dma((2,)), dma((2,)),
            dma((others,)), dma((others,)),
            dma((2,)), dma((2,)),
        ],
        compiler_params=pltpu.CompilerParams(collective_id=0, has_side_effects=True, vmem_limit_bytes=VMEM_LIMIT),
    )(q, k, v, x, top, gains)
    return pl.pallas_call(
        write_kernel,
        out_shape=(out,) * 4,
        in_specs=[pl.BlockSpec(memory_space=pltpu.VMEM)],
        out_specs=(pl.BlockSpec(memory_space=pl.ANY),) * 4,
        scratch_shapes=[dma((4,))],
        compiler_params=pltpu.CompilerParams(vmem_limit_bytes=1 << 20),
    )(outs)


def solution(mesh):
    sizes = (mesh.shape["pp"], mesh.shape["cp"], mesh.shape["tp"])
    part = P("pp", "cp", "tp")
    return jax.shard_map(
        functools.partial(on_device, sizes),
        mesh=mesh,
        in_specs=(part, part, part, part, P("cp", "tp"), P("pp", "tp")),
        out_specs=(part, part, part, part),
        check_vma=False,
    )
```

```python
import functools

import jax
import jax.numpy as jnp
from jax import lax
from jax.experimental import pallas as pl
from jax.experimental.pallas import tpu as pltpu
from jax.sharding import PartitionSpec as P

HEAD = 128
LANES = 128
EPSILON = 1e-06
PIECES = 4
LEAD = 2
SWAPPED = (3, 5, 6)
PACKED = 2
VMEM_LIMIT = 24 << 20
MESH = pl.DeviceIdType.MESH
F32 = jnp.float32
BF16 = jnp.bfloat16


def dot(a, b, a_dim, b_dim):
    return lax.dot_general(a, b, (((a_dim,), (b_dim,)), ((), ())), preferred_element_type=F32)


def swapped_heads(heads):
    return [h for h in SWAPPED if h < heads]


def kernel(
    sizes,
    q_hbm, k_hbm, v_hbm, x_hbm, top_hbm, gain_hbm,
    outs,
    q, k, v, x, top, gain,
    pre_in, pre_out, suf_in, suf_out, states, scores, att, ng, gate, ag, b_out, b_in,
    rows_out, rows_in, inv_out, inv_in, z_out, z_in, mix_out, mix_in, turned,
    in_sem, chain_send, chain_recv,
    b_send, b_recv, row_send, row_recv, inv_send, inv_recv, mix_sem, z_sem,
):
    layers, blocks, shards = sizes
    p = lax.axis_index("pp") if layers > 1 else jnp.int32(0)
    c = lax.axis_index("cp") if blocks > 1 else jnp.int32(0)
    t = lax.axis_index("tp") if shards > 1 else jnp.int32(0)
    rows, width = q.shape
    sec, qg, kg, vg = (outs.at[i] for i in range(4))
    heads = width // HEAD
    padded = rows_out.shape[2]
    swapped = swapped_heads(heads) if layers == 2 else []
    paired = len(swapped) > 0
    order = [h for h in range(heads) if h not in swapped] + swapped
    total_width = width * shards

    def part(i):
        return slice(i * (HEAD // PIECES), (i + 1) * (HEAD // PIECES))

    def cols(h):
        return slice(h * HEAD, (h + 1) * HEAD)

    loads = [
        pltpu.make_async_copy(k_hbm.at[0], k, in_sem.at[0]),
        pltpu.make_async_copy(v_hbm.at[0], v, in_sem.at[1]),
        pltpu.make_async_copy(q_hbm.at[0], q, in_sem.at[2]),
        pltpu.make_async_copy(x_hbm.at[0], x, in_sem.at[3]),
        pltpu.make_async_copy(gain_hbm, gain, in_sem.at[4]),
        pltpu.make_async_copy(top_hbm, top, in_sem.at[5]),
    ]
    barrier = pltpu.get_barrier_semaphore()

    @pl.when(c > 0)
    def _():
        pl.semaphore_signal(barrier, inc=1, device_id={"cp": c - 1}, device_id_type=MESH)

    @pl.when(c < blocks - 1)
    def _():
        pl.semaphore_signal(barrier, inc=1, device_id={"cp": c + 1}, device_id_type=MESH)

    for d in range(1, shards):
        pl.semaphore_signal(
            barrier, inc=1, device_id={"tp": lax.rem(t + d, shards)}, device_id_type=MESH
        )
    for d in range(1, layers):
        pl.semaphore_signal(
            barrier, inc=1, device_id={"pp": lax.rem(p + d, layers)}, device_id_type=MESH
        )

    for load in loads[:2]:
        load.start()

    @pl.when(c == 0)
    def _():
        pre_in[...] = jnp.zeros_like(pre_in)

    @pl.when(c == blocks - 1)
    def _():
        suf_in[...] = jnp.zeros_like(suf_in)

    for d in range(1, layers):

        @pl.when(p + d >= layers)
        def _():
            b_in[d - 1] = jnp.zeros(b_in.shape[1:], b_in.dtype)
            inv_in[d - 1] = jnp.zeros(inv_in.shape[1:], inv_in.dtype)

    def pre_copy(h, i):
        return pltpu.make_async_remote_copy(
            src_ref=pre_out.at[h, part(i)], dst_ref=pre_in.at[h, part(i)],
            send_sem=chain_send.at[0], recv_sem=chain_recv.at[h, i],
            device_id={"cp": c + 1}, device_id_type=MESH,
        )

    def suf_copy(h, i):
        return pltpu.make_async_remote_copy(
            src_ref=suf_out.at[h, part(i)], dst_ref=suf_in.at[h, part(i)],
            send_sem=chain_send.at[1], recv_sem=chain_recv.at[h, i],
            device_id={"cp": c - 1}, device_id_type=MESH,
        )

    def b_copy(d, h):
        return pltpu.make_async_remote_copy(
            src_ref=b_out.at[h], dst_ref=b_in.at[d - 1, h],
            send_sem=b_send.at[d - 1], recv_sem=b_recv.at[d - 1, h],
            device_id={"pp": p - d}, device_id_type=MESH,
        )

    def inv_copy(d):
        return pltpu.make_async_remote_copy(
            src_ref=inv_out, dst_ref=inv_in.at[d - 1],
            send_sem=inv_send.at[d - 1], recv_sem=inv_recv.at[d - 1],
            device_id={"pp": p - d}, device_id_type=MESH,
        )

    def z_copy(j):
        return pltpu.make_async_remote_copy(
            src_ref=z_out.at[j], dst_ref=z_in.at[j],
            send_sem=z_sem.at[0], recv_sem=z_sem.at[1],
            device_id={"pp": p + 1}, device_id_type=MESH,
        )

    def z_all():
        return pltpu.make_async_remote_copy(
            src_ref=z_out, dst_ref=z_in,
            send_sem=z_sem.at[0], recv_sem=z_sem.at[1],
            device_id={"pp": p + 1}, device_id_type=MESH,
        )

    def mix_copy(e):
        return pltpu.make_async_remote_copy(
            src_ref=mix_out, dst_ref=mix_in.at[e],
            send_sem=mix_sem.at[0], recv_sem=mix_sem.at[1],
            device_id={"pp": p - 1, "tp": lax.rem(t + e, shards)}, device_id_type=MESH,
        )

    def mix_all():
        return pltpu.make_async_remote_copy(
            src_ref=mix_in, dst_ref=mix_in,
            send_sem=mix_sem.at[0], recv_sem=mix_sem.at[1],
            device_id={"pp": p - 1}, device_id_type=MESH,
        )

    def row_copy(i, d):
        return pltpu.make_async_remote_copy(
            src_ref=rows_out.at[i], dst_ref=rows_in.at[i, d - 1],
            send_sem=row_send.at[i], recv_sem=row_recv.at[i],
            device_id={"tp": lax.rem(t + d, shards)}, device_id_type=MESH,
        )

    def to_row(partial):
        if padded > rows:
            fill = jnp.zeros((padded - rows, LANES), F32)
            partial = jnp.concatenate([partial, fill], axis=0)
        return jnp.broadcast_to(jnp.sum(partial.T, axis=0, keepdims=True), (PACKED, padded))

    def to_col(row):
        return jnp.broadcast_to(row[0:1], (LANES, padded)).T[:rows]

    def row_start(i, partials):
        ids = lax.broadcasted_iota(jnp.int32, (PACKED, padded), 0)
        packed = to_row(partials[0])
        for j in range(1, len(partials)):
            packed = jnp.where(ids == j, to_row(partials[j]), packed)
        rows_out[i] = packed
        for d in range(1, shards):
            row_copy(i, d).start()

    def row_all(i):
        return pltpu.make_async_remote_copy(
            src_ref=rows_in.at[i], dst_ref=rows_in.at[i],
            send_sem=row_send.at[i], recv_sem=row_recv.at[i],
            device_id={"tp": lax.rem(t + 1, shards)}, device_id_type=MESH,
        )

    def row_finish(i):
        total = rows_out[i]
        if shards > 1:
            row_all(i).wait_recv()
        for d in range(1, shards):
            total = total + rows_in[i, d - 1]
        return total

    def row_sent(i):
        if shards > 1:
            row_all(i).wait_send()

    causal = lax.broadcasted_iota(jnp.int32, (rows, rows), 0) >= lax.broadcasted_iota(
        jnp.int32, (rows, rows), 1
    )

    def relay(copy, arrived, sent, h, inner):
        @pl.when(inner)
        def _():
            for i in range(PIECES):
                copy(h, i).wait_recv()
                total = arrived[h, part(i)].astype(F32) + states[h, part(i)]
                sent[h, part(i)] = total.astype(BF16)
                copy(h, i).start()

    def absorb(copy, h, outer):
        @pl.when(outer)
        def _():
            for i in range(PIECES):
                copy(h, i).wait_recv()

    def first(copy, sent, h):
        for i in range(PIECES):
            sent[h, part(i)] = states[h, part(i)].astype(BF16)
            copy(h, i).start()

    def local(h):
        query, value = q[:, cols(h)], v[:, cols(h)]
        score = jnp.where(causal, dot(query, k[:, cols(h)], 1, 1), 0.0).astype(BF16)
        scores[h] = score
        att[:, cols(h)] = dot(score, value, 1, 0)
        gate[:, cols(h)] = jax.nn.sigmoid(x[:, cols(h)].astype(F32))

    loads[0].wait()
    loads[1].wait()
    for load in loads[2:]:
        load.start()
    states[0] = dot(k[:, cols(0)], v[:, cols(0)], 0, 0)
    partners = (shards - 1) + (layers - 1)
    pl.semaphore_wait(
        barrier, partners + jnp.where(c > 0, 1, 0) + jnp.where(c < blocks - 1, 1, 0)
    )
    for h in range(heads):
        if h > 0:
            states[h] = dot(k[:, cols(h)], v[:, cols(h)], 0, 0)
        if blocks > 1:

            @pl.when(c == 0)
            def _():
                first(pre_copy, pre_out, h)

    for load in loads[2:]:
        load.wait()
    lead = min(LEAD, heads) if blocks > 1 else heads
    for h in range(lead):
        local(h)
    if lead < heads:

        @pl.when(c != 1)
        def _():
            for h in range(lead, heads):
                local(h)

    merged = layers == 1 or paired
    squares = jnp.zeros((rows, LANES), F32)
    firsts = jnp.zeros((rows, LANES), F32)
    for h in range(heads):
        if blocks > 1:
            relay(pre_copy, pre_in, pre_out, h, (c > 0) & (c < blocks - 1))
            absorb(pre_copy, h, (c > 0) & (c == blocks - 1))
        attention = att[:, cols(h)] + dot(q[:, cols(h)], pre_in[h], 1, 0)
        att[:, cols(h)] = attention
        squares = squares + attention * attention
        sig = gate[:, cols(h)]
        if merged:
            weighted = top[:, cols(h)].astype(F32) * (gain[:, cols(h)] * sig)
            ng[:, cols(h)] = weighted
            firsts = firsts + weighted * attention
        if layers > 1:
            b_out[h] = (attention * (gain[:, cols(h)] * sig * (1.0 - sig))).astype(BF16)
        if h in swapped:

            @pl.when(p == 0)
            def _():
                z_out[swapped.index(h)] = (weighted * attention).astype(BF16)
                z_copy(swapped.index(h)).start()

        else:
            for d in range(1, layers):

                @pl.when(p >= d)
                def _():
                    b_copy(d, h).start()

        if h + lead < heads:

            @pl.when(c == 1)
            def _():
                local(h + lead)

    row_start(0, (squares, firsts))
    for h in range(heads):
        turned[h] = q[:, cols(h)].T
    if paired:

        @pl.when(p == 1)
        def _():
            seconds = jnp.zeros((rows, LANES), F32)
            z_all().wait_recv()
            for j, h in enumerate(swapped):
                seconds = seconds + z_in[j].astype(F32) * b_out[h].astype(F32)
            ids = lax.broadcasted_iota(jnp.int32, (PACKED, padded), 0)
            mix_out[...] = jnp.where(ids == 1, to_row(seconds), rows_out[0])
            for e in range(shards):
                mix_copy(e).start()

    sums = row_finish(0)
    if paired:

        @pl.when(p == 1)
        def _():
            for h in swapped:
                b_copy(1, h).start()

    inv_row = 1.0 / jnp.sqrt(sums[0:1] / total_width + EPSILON)
    if not paired:
        inv_out[...] = jnp.broadcast_to(inv_row, inv_out.shape)
        for d in range(1, layers):

            @pl.when(p >= d)
            def _():
                inv_copy(d).start()

    inv = to_col(inv_row)

    def wait_inv():
        for d in range(1, layers):

            @pl.when(p + d < layers)
            def _():
                inv_copy(d).wait_recv()

    def wait_b(some):
        for d in range(1, layers):

            @pl.when(p + d < layers)
            def _():
                for h in some:
                    b_copy(d, h).wait_recv()

    def later(h, later_inv):
        incoming = top[:, cols(h)].astype(F32)
        for d in range(1, layers):
            incoming = incoming * (1.0 + b_in[d - 1, h].astype(F32) * later_inv[d - 1])
        return incoming

    if merged:
        mean_row = sums[1:2]
        later_inv = []
        if paired:

            @pl.when(p == 0)
            def _():
                seconds = jnp.zeros((rows, LANES), F32)
                for h in order:
                    if h not in swapped:
                        wait_b([h])
                        seconds = seconds + ng[:, cols(h)] * att[:, cols(h)] * b_in[0, h].astype(F32)
                row_start(1, (seconds,))
                mix_all().wait_recv()
                total = mix_in[0]
                for e in range(1, shards):
                    total = total + mix_in[e]
                above = 1.0 / jnp.sqrt(total[0:1] / total_width + EPSILON)
                inv_in[0] = jnp.broadcast_to(above, inv_in.shape[1:])
                inv_out[...] = jnp.broadcast_to(total[1:2], inv_out.shape)

            later_inv = [to_col(inv_in[0])]
        for h in order:
            if h not in swapped:
                scaled = ng[:, cols(h)] * inv
                if paired:
                    scaled = scaled * (1.0 + b_in[0, h].astype(F32) * later_inv[0])
                ng[:, cols(h)] = scaled
        if paired:

            @pl.when(p == 0)
            def _():
                total = row_finish(1)
                row_sent(1)
                rows_out[1] = jnp.broadcast_to(total[0:1] + inv_out[0:1], rows_out.shape[1:])

            @pl.when(p == 1)
            def _():
                rows_out[1] = jnp.zeros(rows_out.shape[1:], F32)

            mean_row = mean_row + inv_in[0, 0:1] * rows_out[1, 0:1]
        mean_row = mean_row * inv_row
    else:
        wait_inv()
        later_inv = [to_col(inv_in[d - 1]) for d in range(1, layers)]
        products = jnp.zeros((rows, LANES), F32)
        for h in range(heads):
            wait_b([h])
            weighted = later(h, later_inv) * (gain[:, cols(h)] * gate[:, cols(h)])
            ng[:, cols(h)] = weighted
            products = products + weighted * att[:, cols(h)] * inv
        row_start(1, (products,))
        mean_row = row_finish(1)
    scale = to_col(mean_row / total_width * inv_row * inv_row)
    for h in order:
        scaled = ng[:, cols(h)]
        if not merged:
            scaled = scaled * inv
        if h in swapped:
            wait_b([h])
            scaled = scaled * inv * (1.0 + b_in[0, h].astype(F32) * later_inv[0])
        grad = (scaled - att[:, cols(h)] * scale).astype(BF16)
        ag[:, cols(h)] = grad
        states[h] = dot(turned[h], grad, 1, 0)
        if blocks > 1:

            @pl.when(c == blocks - 1)
            def _():
                first(suf_copy, suf_out, h)

    def inner_grads(h):
        sig = gate[:, cols(h)]
        slope = gain[:, cols(h)] * sig * (1.0 - sig)
        factor = 1.0 + att[:, cols(h)] * inv * slope
        sec[:, cols(h)] = (later(h, later_inv) * factor).astype(BF16)
        query, key, value = q[:, cols(h)], k[:, cols(h)], v[:, cols(h)]
        grad = ag[:, cols(h)]
        score_grad = jnp.where(causal, dot(grad, value, 1, 1), 0.0).astype(BF16)
        query_grad = dot(score_grad, key, 1, 0) + dot(grad, pre_in[h], 1, 1)
        qg[:, cols(h)] = query_grad.astype(BF16)
        att[:, cols(h)] = dot(score_grad, query, 0, 0)
        ng[:, cols(h)] = dot(scores[h], grad, 0, 0)

    for h in order:
        inner_grads(h)
    for h in order:
        if blocks > 1:
            relay(suf_copy, suf_in, suf_out, h, (c < blocks - 1) & (c > 0))
    for h in order:
        if blocks > 1:
            absorb(suf_copy, h, (c < blocks - 1) & (c == 0))
        suffix = suf_in[h]
        key_grad = att[:, cols(h)] + dot(v[:, cols(h)], suffix, 1, 1)
        kg[:, cols(h)] = key_grad.astype(BF16)
        value_grad = ng[:, cols(h)] + dot(k[:, cols(h)], suffix, 1, 0)
        vg[:, cols(h)] = value_grad.astype(BF16)

    if blocks > 1:

        @pl.when(c < blocks - 1)
        def _():
            pltpu.make_async_remote_copy(
                src_ref=pre_out, dst_ref=pre_in,
                send_sem=chain_send.at[0], recv_sem=chain_recv.at[0, 0],
                device_id={"cp": c + 1}, device_id_type=MESH,
            ).wait_send()

        @pl.when(c > 0)
        def _():
            pltpu.make_async_remote_copy(
                src_ref=suf_out, dst_ref=suf_in,
                send_sem=chain_send.at[1], recv_sem=chain_recv.at[0, 0],
                device_id={"cp": c - 1}, device_id_type=MESH,
            ).wait_send()

    for d in range(1, layers):

        @pl.when(p >= d)
        def _():
            if paired:
                mix_all().wait_send()
            else:
                inv_copy(d).wait_send()
            pltpu.make_async_remote_copy(
                src_ref=b_out, dst_ref=b_in.at[d - 1],
                send_sem=b_send.at[d - 1], recv_sem=b_recv.at[d - 1, 0],
                device_id={"pp": p - d}, device_id_type=MESH,
            ).wait_send()

    if swapped:

        @pl.when(p == 0)
        def _():
            z_all().wait_send()

    row_sent(0)
    if not merged:
        row_sent(1)


def write_kernel(outs, sec_hbm, qg_hbm, kg_hbm, vg_hbm, sem):
    rows = outs.shape[1]
    step = rows // 4 if rows % 32 == 0 else rows
    dsts = (sec_hbm, qg_hbm, kg_hbm, vg_hbm)
    for i, dst in enumerate(dsts):
        for r in range(0, rows, step):
            pltpu.make_async_copy(
                outs.at[i, r : r + step], dst.at[0, r : r + step], sem.at[i]
            ).start()
    for i, dst in enumerate(dsts):
        pltpu.make_async_copy(outs.at[i], dst.at[0], sem.at[i]).wait()


def on_device(sizes, q, k, v, x, top, gains):
    layers, blocks, shards = sizes
    rows, width = q.shape[1:]
    heads = width // HEAD
    padded = -(-rows // LANES) * LANES
    others, peers = max(layers - 1, 1), max(shards - 1, 1)
    swaps = max(len(swapped_heads(heads)), 1)
    wide = pltpu.VMEM((rows, width), BF16)
    wide32 = pltpu.VMEM((rows, width), F32)
    square = pltpu.VMEM((heads, HEAD, HEAD), BF16)
    dma = pltpu.SemaphoreType.DMA
    out = jax.ShapeDtypeStruct((1, rows, width), BF16)
    q, k, v, x, top, gains = (
        pltpu.with_memory_space_constraint(a, pltpu.HBM) for a in (q, k, v, x, top, gains)
    )
    outs = pl.pallas_call(
        functools.partial(kernel, sizes),
        out_shape=jax.ShapeDtypeStruct((4, rows, width), BF16),
        in_specs=[pl.BlockSpec(memory_space=pltpu.HBM)] * 6,
        out_specs=pl.BlockSpec(memory_space=pltpu.VMEM),
        scratch_shapes=[
            wide, wide, wide, wide, wide, pltpu.VMEM((1, width), F32),
            square, square, square, square,
            pltpu.VMEM((heads, HEAD, HEAD), F32),
            pltpu.VMEM((heads, rows, rows), BF16),
            wide32, wide32, wide32, wide,
            pltpu.VMEM((heads, rows, HEAD), BF16),
            pltpu.VMEM((others, heads, rows, HEAD), BF16),
            pltpu.VMEM((2, PACKED, padded), F32),
            pltpu.VMEM((2, peers, PACKED, padded), F32),
            pltpu.VMEM((8, padded), F32),
            pltpu.VMEM((others, 8, padded), F32),
            pltpu.VMEM((swaps, rows, HEAD), BF16),
            pltpu.VMEM((swaps, rows, HEAD), BF16),
            pltpu.VMEM((PACKED, padded), F32),
            pltpu.VMEM((shards, PACKED, padded), F32),
            pltpu.VMEM((heads, HEAD, rows), BF16),
            dma((6,)),
            dma((2,)), dma((heads, PIECES)),
            dma((others,)), dma((others, heads)),
            dma((2,)), dma((2,)),
            dma((others,)), dma((others,)),
            dma((2,)), dma((2,)),
        ],
        compiler_params=pltpu.CompilerParams(collective_id=0, has_side_effects=True, vmem_limit_bytes=VMEM_LIMIT),
    )(q, k, v, x, top, gains)
    return pl.pallas_call(
        write_kernel,
        out_shape=(out,) * 4,
        in_specs=[pl.BlockSpec(memory_space=pltpu.VMEM)],
        out_specs=(pl.BlockSpec(memory_space=pl.ANY),) * 4,
        scratch_shapes=[dma((4,))],
        compiler_params=pltpu.CompilerParams(vmem_limit_bytes=1 << 20),
    )(outs)


def solution(mesh):
    sizes = (mesh.shape["pp"], mesh.shape["cp"], mesh.shape["tp"])
    part = P("pp", "cp", "tp")
    return jax.shard_map(
        functools.partial(on_device, sizes),
        mesh=mesh,
        in_specs=(part, part, part, part, P("cp", "tp"), P("pp", "tp")),
        out_specs=(part, part, part, part),
        check_vma=False,
    )
```
